32 devices in a mesh: groups: 2 (over x), node: 8 (over z, y), rep: 2 (over core).
Axes of the slice: x: 2, y: 2, z: 4, core: 2. Of those that a mesh axis runs over, the one named last changes fastest.
Arguments:
- normed_input: bfloat16 [4, 1024, 5120], P(('groups', 'rep'), 'node'), parts along dimension 0, may hold values from -6 to 6
- queries: bfloat16 [4, 1024, 2560], P(('groups', 'rep'), 'node'), parts along dimension 0, may hold values from -120 to 120
- rotated_key_heads: bfloat16 [4, 1024, 512], P(('groups', 'rep'), 'node'), parts along dimension 0, may hold values from -6 to 6
- frozen_value_rows: bfloat16 [4, 1024, 512], P(('groups', 'rep'), 'node'), parts along dimension 0, may hold values from -6 to 6
- adapter_down_weight: bfloat16 [5120, 32], replicated, may hold values from -0.078125 to 0.078125
- adapter_up_weight: bfloat16 [32, 512], replicated, may hold values from -1 to 1
- output_gradient: bfloat16 [4, 1024, 2560], P(('groups', 'rep'), 'node'), parts along dimension 0, may hold values from -6 to 6
- parents: int32 [4, 8], P(('groups', 'rep')), parts along dimension 0, may hold values from -1 to 6, as said below
- lengths: int32 [4, 8], P(('groups', 'rep')), parts along dimension 0, may hold values from 32 to 128, as said below
Outputs:
- attended: bfloat16 [4, 1024, 2560], P(('groups', 'rep'), 'node'), parts along dimension 0
- query_grad: bfloat16 [4, 1024, 2560], P(('groups', 'rep'), 'node'), parts along dimension 0
- down_grad: float32 [10240, 32], P('groups'), parts along dimension 0
- up_grad: float32 [64, 512], P('groups'), parts along dimension 0
The draws below stay inside these ranges and needn't reach their ends.
There are 2 independent parts, one for each index of `groups`. The reference program is written for one: setup_inputs(seed, part) draws one part's arguments, and reference() takes and returns one part's arrays. A program takes and returns all parts, laid end to end along the dimension named above; an argument that names none is the same for every part. Nothing has to cross between parts.
Inputs may be any that keep to these rules, and one draw needn't show every extreme that they name: `parents`: slots 0 to 1 form the shared prompt, each the parent of the next, slot 0 the root. Every other slot's parent is slot 1 or a slot below it, and every ancestor of a slot s outside the prompt lies among the slots s - 5 to s - 1. `lengths`: prompt blocks are full.
All inputs are finite; a program needn't handle non-finite values.
Results may differ from the reference program's by a relative error of at most 0.0062.
Values may be sent and summed in bfloat16 or wider, within the bound.
No kernel may reach another device: no remote copies, remote signals or barrier semaphores. Data moves between devices by JAX's collectives and lax.ppermute only.
A program may use at most 128 MiB of HBM per device.

```python
import jax
import jax.numpy as jnp
from jax import lax

MODEL_WIDTH = 5120
HQ = 20
KEY_HEADS = 4
HEAD_SIZE = 128
ADAPTER_RANK = 32
BLK = 128
PROMPT = 2
SPAN = 5
TREES = 2
ROWS = 1024
N_NODE = 8
N_REP = 2


def tree_links(tree_key):
    position_index = jnp.arange(N_NODE, dtype=jnp.int32)
    order_scores = jax.random.randint(tree_key, (N_NODE, N_NODE), 0, 1024, dtype=jnp.int32)
    start = jnp.where(position_index < PROMPT, position_index - 1, 0).astype(jnp.int32)

    def extend(carried, tree_position):
        parent_row, lowest = carried
        permitted_mask = (position_index == PROMPT - 1) | (position_index >= PROMPT) & (position_index < tree_position) & (position_index >= tree_position - SPAN) & (lowest >= tree_position - SPAN)
        extra_logit = jnp.where(position_index == tree_position - 1, 400, 0).astype(jnp.int32)
        sorted_order = jnp.where(permitted_mask, (order_scores[tree_position] + extra_logit) * 64 + position_index, -1)
        chosen = jnp.argmax(sorted_order).astype(jnp.int32)
        parent_row = parent_row.at[tree_position].set(chosen)
        lowest = lowest.at[tree_position].set(jnp.where(chosen == PROMPT - 1, tree_position, lowest[chosen]).astype(jnp.int32))
        return ((parent_row, lowest), None)
    (parent_row, lowest), unused = lax.scan(extend, (start, position_index), jnp.arange(PROMPT, N_NODE, dtype=jnp.int32))
    return parent_row


def draw_parents(key, part):
    tree_keys = jax.random.split(jax.random.fold_in(key, 5), N_REP)
    return jax.vmap(tree_links)(tree_keys).astype(jnp.int32)


def draw_lengths(key, part):
    drawn = jax.random.randint(jax.random.fold_in(key, 7), (N_REP, N_NODE), BLK // 4, BLK + 1, dtype=jnp.int32)
    position_index = jnp.arange(N_NODE, dtype=jnp.int32)[None, :]
    drawn = jnp.where(position_index < PROMPT, BLK, drawn)
    drawn = jnp.where(position_index == PROMPT, BLK // 4, drawn)
    return drawn.astype(jnp.int32)


def key_table(key):
    table = jnp.clip(jax.random.normal(jax.random.fold_in(key, 11), (N_REP, N_NODE * BLK, KEY_HEADS * HEAD_SIZE), jnp.float32), -5.0, 5.0)
    return table


def draw_rotated_key_heads(key, part):
    return key_table(key).astype(jnp.bfloat16)


def draw_queries(key, part):
    entries = jnp.clip(jax.random.normal(jax.random.fold_in(key, 13), (N_REP, N_NODE * BLK, HQ * HEAD_SIZE), jnp.float32), -5.0, 5.0)
    return entries.astype(jnp.bfloat16)


def steps_of(rng, extent, cuts, low, largest):
    loudness, own = 1.0, jax.random.fold_in(rng, 6)
    for dim, blocks in cuts:
        heights = jnp.exp(jax.random.uniform(jax.random.fold_in(own, dim), (blocks,), jnp.float32, low / len(cuts), largest / len(cuts)))
        loudness = loudness * jnp.repeat(heights, extent[dim] // blocks).reshape([-1 if axis == dim else 1 for axis in range(len(extent))])
    return loudness


def normal_values(rng, dims, deviation, most, pieces=(), kind=jnp.bfloat16):
    values = deviation * jax.random.normal(rng, dims, jnp.float32)
    if pieces:
        values = values * steps_of(rng, dims, pieces, -0.22, 0.18)
    return jnp.clip(values, -most, most).astype(kind)


def setup_inputs(seed: int = 0, part: int = 0) -> dict:
    key_of = jax.random.split(jax.random.key(seed), 10)
    part_splits = jax.random.split(jax.random.fold_in(key_of[9], part), 10)
    normed_input = normal_values(part_splits[0], (TREES, ROWS, MODEL_WIDTH), 1.0, 6.0, ((0, 2), (1, 8)))
    queries = draw_queries(jax.random.fold_in(jax.random.fold_in(key_of[9], part), 71), part)
    rotated_key_heads = draw_rotated_key_heads(jax.random.fold_in(jax.random.fold_in(key_of[9], part), 71), part)
    frozen_value_rows = normal_values(part_splits[3], (TREES, ROWS, KEY_HEADS * HEAD_SIZE), 1.0, 6.0, ((0, 2), (1, 8)))
    adapter_down_weight = normal_values(key_of[4], (MODEL_WIDTH, ADAPTER_RANK), MODEL_WIDTH ** -0.5, 0.078125)
    adapter_up_weight = normal_values(key_of[5], (ADAPTER_RANK, KEY_HEADS * HEAD_SIZE), ADAPTER_RANK ** -0.5, 1.0)
    output_gradient = normal_values(part_splits[6], (TREES, ROWS, HQ * HEAD_SIZE), 1.0, 6.0, ((0, 2), (1, 8)))
    parents = draw_parents(jax.random.fold_in(jax.random.fold_in(key_of[9], part), 71), part)
    lengths = draw_lengths(jax.random.fold_in(jax.random.fold_in(key_of[9], part), 71), part)
    return dict(normed_input=normed_input, queries=queries, rotated_key_heads=rotated_key_heads, frozen_value_rows=frozen_value_rows, adapter_down_weight=adapter_down_weight, adapter_up_weight=adapter_up_weight, output_gradient=output_gradient, parents=parents, lengths=lengths)


NEGATIVE = -1.0e30
HIGHEST = lax.Precision.HIGHEST


def chain_of(parent_row):
    current = parent_row
    columns = []
    for height in range(PROMPT + SPAN):
        columns.append(current)
        current = jnp.where(current >= 0, parent_row[jnp.maximum(current, 0)], -1).astype(jnp.int32)
    return jnp.stack(columns, 1)


def reference(normed_input, queries, rotated_key_heads, frozen_value_rows, adapter_down_weight, adapter_up_weight, output_gradient, parents, lengths):
    trees = normed_input.shape[0]
    slot_count = parents.shape[1]
    block_rows = normed_input.shape[1] // slot_count
    groups_per = HQ // KEY_HEADS
    key_value_width = KEY_HEADS * HEAD_SIZE
    inverse_root = HEAD_SIZE ** -0.5
    position = jnp.arange(block_rows, dtype=jnp.int32)
    adapter_inner = jnp.dot(normed_input.reshape(-1, MODEL_WIDTH), adapter_down_weight, preferred_element_type=jnp.float32).astype(jnp.bfloat16)
    value_rows = frozen_value_rows.reshape(-1, key_value_width).astype(jnp.float32) + jnp.dot(adapter_inner, adapter_up_weight, preferred_element_type=jnp.float32)
    value_rows = value_rows.astype(jnp.bfloat16).reshape(trees, slot_count, block_rows, KEY_HEADS, HEAD_SIZE)
    adapter_inner = adapter_inner.reshape(trees, slot_count * block_rows, ADAPTER_RANK)
    up_weight_float = adapter_up_weight.astype(jnp.float32)
    count = 1 + PROMPT + SPAN
    not_first = (jnp.arange(count, dtype=jnp.int32) > 0)[:, None, None]
    causal = position[None, :] <= position[:, None]
    down_total = jnp.zeros((MODEL_WIDTH, ADAPTER_RANK), jnp.float32)
    up_total = jnp.zeros((ADAPTER_RANK, key_value_width), jnp.float32)
    attended_all = []
    grads_all = []
    for tree in range(trees):
        own_ids = jnp.arange(slot_count, dtype=jnp.int32)[:, None]
        cand_ids = jnp.concatenate([own_ids, chain_of(parents[tree])], 1).astype(jnp.int32)
        safe_ids = jnp.maximum(cand_ids, 0).astype(jnp.int32)
        keys_tree = rotated_key_heads[tree].reshape(slot_count, block_rows, KEY_HEADS, HEAD_SIZE).astype(jnp.float32)
        values_tree = value_rows[tree].astype(jnp.float32)
        query_tree = queries[tree].reshape(slot_count, block_rows, KEY_HEADS, groups_per, HEAD_SIZE).astype(jnp.float32)
        grad_tree = output_gradient[tree].reshape(slot_count, block_rows, KEY_HEADS, groups_per, HEAD_SIZE)
        length_row = lengths[tree]

        def slot_work(tree_position):
            picked = safe_ids[tree_position]
            usable = cand_ids[tree_position] >= 0
            keys_here = keys_tree[picked]
            values_here = values_tree[picked]
            key_live = position[None, :] < length_row[picked][:, None]
            permitted_mask = (causal[None] | not_first) & key_live[:, None, :] & usable[:, None, None]
            logits = jnp.einsum("ikgd,cjkd->ckgij", query_tree[tree_position], keys_here, precision=HIGHEST) * inverse_root
            logits = jnp.where(permitted_mask[:, None, None], logits, NEGATIVE)
            highest = jnp.max(logits, axis=(0, 4))
            totals = jnp.sum(jnp.exp(logits - highest[None, :, :, :, None]), axis=(0, 4))
            log_total = highest + jnp.log(totals)
            weights = jnp.exp(logits - log_total[None, :, :, :, None])
            rounded = lax.optimization_barrier(weights.astype(jnp.bfloat16)).astype(jnp.float32)
            output = jnp.einsum("ckgij,cjkd->ikgd", rounded, values_here, precision=HIGHEST)
            live = position < length_row[tree_position]
            attended = jnp.where(live[:, None, None, None], output, 0.0).astype(jnp.bfloat16)
            head_gradient = jnp.where(live[:, None, None, None], grad_tree[tree_position], jnp.zeros_like(grad_tree[tree_position])).astype(jnp.float32)
            row_dots = jnp.einsum("ikgd,ikgd->kgi", head_gradient, output, precision=HIGHEST)
            pressure = jnp.einsum("ikgd,cjkd->ckgij", head_gradient, values_here, precision=HIGHEST)
            slopes = (weights * (pressure - row_dots[None, :, :, :, None]) * inverse_root).astype(jnp.bfloat16)
            slopes = lax.optimization_barrier(slopes).astype(jnp.float32)
            query_grad = jnp.einsum("ckgij,cjkd->ikgd", slopes, keys_here, precision=HIGHEST).astype(jnp.bfloat16)
            value_parts = jnp.einsum("ckgij,ikgd->cjkd", rounded, head_gradient, precision=HIGHEST)
            return attended, query_grad, value_parts

        attended, query_grad, value_parts = lax.map(slot_work, jnp.arange(slot_count, dtype=jnp.int32))
        value_total = jnp.zeros((slot_count, block_rows, KEY_HEADS, HEAD_SIZE), jnp.float32)
        value_total = value_total.at[safe_ids.reshape(-1)].add(value_parts.reshape(-1, block_rows, KEY_HEADS, HEAD_SIZE))
        value_flat = value_total.reshape(-1, key_value_width)
        projected = jnp.dot(value_flat, up_weight_float.T, precision=HIGHEST).astype(jnp.bfloat16)
        down_total = down_total + jnp.dot(normed_input[tree].T, projected, preferred_element_type=jnp.float32)
        up_total = up_total + jnp.dot(adapter_inner[tree].astype(jnp.float32).T, value_flat, precision=HIGHEST)
        attended_all.append(attended.reshape(slot_count * block_rows, HQ * HEAD_SIZE))
        grads_all.append(query_grad.reshape(slot_count * block_rows, HQ * HEAD_SIZE))
    factor = (trees * slot_count * block_rows) ** -0.5
    return jnp.stack(attended_all), jnp.stack(grads_all), down_total * factor, up_total * factor
```

```python
import functools

import jax
import jax.numpy as jnp
from jax import lax
from jax.experimental import pallas as pl
from jax.experimental.pallas import tpu as pltpu
from jax.sharding import PartitionSpec as P

HQ = 20
KEY_HEADS = 4
HEAD_SIZE = 128
PROMPT = 2
SPAN = 5
PER = HQ // KEY_HEADS

NEGATIVE = -1e30
LOG2E = 1.4426950408889634
F32 = jnp.float32
BF16 = jnp.bfloat16


VMEM_LIMIT = 56 * 1024 * 1024


def dot(a, b):
    return lax.dot_general(a, b, (((1,), (0,)), ((), ())), preferred_element_type=F32)


def dot_nt(a, b):
    return lax.dot_general(a, b, (((1,), (1,)), ((), ())), preferred_element_type=F32)


def dot_tn(a, b):
    return lax.dot_general(a, b, (((0,), (0,)), ((), ())), preferred_element_type=F32)


def paired(slots):
    return slots % 2 == 0 and slots <= 1 + PROMPT + SPAN


def candidate_count(slots):
    return slots if paired(slots) else 1 + PROMPT + SPAN


def candidate_slot(slots, own, c):
    if paired(slots):
        pair = own - (c // 2) * 2
        slot = pair + (c % 2) * (1 - 2 * (pair % 2))
        return jnp.where(pair >= 0, slot, -1)
    window = own - c
    window = jnp.where(window >= PROMPT, window, -1)
    prompt = c - SPAN - 1
    prompt = jnp.where(prompt < own, prompt, -1)
    return jnp.where(c == 0, own, jnp.where(c <= SPAN, window, prompt))


def mark_candidates(slots, parents_ref, lengths_ref, live_ref):
    own = lax.axis_index("node")
    count = candidate_count(slots)
    for c in range(count):
        live_ref[c] = 0
    live_ref[0] = lengths_ref[0, own]

    def climb(step, current):
        at = jnp.maximum(current, 0)
        for c in range(1, count):
            slot = candidate_slot(slots, own, c)

            @pl.when((slot == current) & (current >= 0))
            def _():
                live_ref[c] = lengths_ref[0, at]

        return jnp.where(current >= 0, parents_ref[0, at], -1)

    lax.fori_loop(0, PROMPT + SPAN, climb, parents_ref[0, own])


def prepare_kernel(
    lengths_ref, x_ref, down_ref, up_ref, frozen_ref, q_ref, g_ref,
    message_ref, qt_ref, gt_ref, gs_ref,
):
    own = lax.axis_index("node")
    rows = x_ref.shape[0]
    width = frozen_ref.shape[1]
    low_t = dot_nt(down_ref[...], x_ref[...]).astype(BF16)
    values = frozen_ref[...].astype(F32) + dot_tn(low_t, up_ref[...])
    message_ref[:rows, :] = values.astype(BF16)
    half = low_t.shape[0] // 2
    message_ref[rows:, :] = jnp.zeros((half, width), BF16)
    message_ref[rows:, :rows] = low_t[:half]
    message_ref[rows:, rows : 2 * rows] = low_t[half:]
    length = lengths_ref[0, own]
    live = lax.broadcasted_iota(jnp.int32, (rows, HEAD_SIZE), 0) < length
    for h in range(HQ):
        cols = slice(h * HEAD_SIZE, (h + 1) * HEAD_SIZE)
        here = slice(h * rows, (h + 1) * rows)
        qt_ref[:, here] = q_ref[:, cols].T
        g = jnp.where(live, g_ref[:, cols].astype(F32), 0.0).astype(BF16)
        gs_ref[here, :] = g
        gt_ref[:, here] = g.T


def prepare(lengths, x, down_t, up, frozen, q, g):
    rows = x.shape[0]
    rank, width = up.shape
    vm = pl.BlockSpec(memory_space=pltpu.VMEM)
    return pl.pallas_call(
        prepare_kernel,
        name="prepare",
        out_shape=(
            jax.ShapeDtypeStruct((rows + rank // 2, width), BF16),
            jax.ShapeDtypeStruct((HEAD_SIZE, HQ * rows), BF16),
            jax.ShapeDtypeStruct((HEAD_SIZE, HQ * rows), BF16),
            jax.ShapeDtypeStruct((HQ * rows, HEAD_SIZE), BF16),
        ),
        in_specs=[pl.BlockSpec(memory_space=pltpu.SMEM)] + [vm] * 6,
        out_specs=(vm,) * 4,
        compiler_params=pltpu.CompilerParams(vmem_limit_bytes=VMEM_LIMIT),
        cost_estimate=pl.CostEstimate(flops=100_000_000, bytes_accessed=6_000_000, transcendentals=0),
    )(lengths, x, down_t, up, frozen, q, g)


def stats_kernel(slots, scale, *refs):
    count = candidate_count(slots)
    parents_ref, lengths_ref = refs[:2]
    key_refs = refs[2 : 2 + count]
    qt_ref, gs_ref, up_ref = refs[2 + count : 5 + count]
    proj_ref, part_ref, lse_ref = refs[5 + count : 8 + count]
    live_ref, keys, weights, tops, acc = refs[8 + count :]
    group = pl.program_id(0)
    rows = key_refs[0].shape[0]
    lanes = PER * rows
    own = lax.axis_index("node")

    @pl.when(group == 0)
    def _():
        mark_candidates(slots, parents_ref, lengths_ref, live_ref)
        acc[...] = jnp.zeros_like(acc)

    for c in range(count):
        keys[c] = key_refs[c][...]
    key_at = lax.broadcasted_iota(jnp.int32, (rows, rows), 0)
    query_at = lax.broadcasted_iota(jnp.int32, (rows, rows), 1)
    qt = qt_ref[...]

    def scores(c, allowed):
        s = dot(keys[c], qt)
        return jnp.concatenate(
            [jnp.where(allowed, s[:, i * rows : (i + 1) * rows], NEGATIVE) for i in range(PER)], axis=1
        )

    s = scores(0, (key_at <= query_at) & (key_at < live_ref[0]))
    top = jnp.max(s, axis=0, keepdims=True)
    p = jnp.exp2(s * scale - top * scale)
    total = jnp.sum(p, axis=0, keepdims=True)
    weights[0] = p
    tops[0] = top

    def first(c, carried):
        def update(current):
            top, total = current
            s = scores(c, key_at < live_ref[c])
            raised = jnp.maximum(top, jnp.max(s, axis=0, keepdims=True))
            p = jnp.exp2(s * scale - raised * scale)
            weights[c] = p
            tops[c] = raised
            total = total * jnp.exp2((top - raised) * scale) + jnp.sum(p, axis=0, keepdims=True)
            return raised, total

        return lax.cond(live_ref[c] > 0, update, lambda current: current, carried)

    top, total = lax.fori_loop(1, count, first, (top, total))
    lse_ref[...] = top * scale + jnp.log2(total)
    inverse = 1.0 / total
    gs = gs_ref[...]
    up = up_ref[...]

    def second(c, carried):
        @pl.when(live_ref[c] > 0)
        def _():
            factor = jnp.exp2((tops[c] - top) * scale) * inverse
            w = (weights[c] * factor).astype(BF16)
            part = dot(w, gs)
            high = part.astype(BF16)
            rest = (part - high.astype(F32)).astype(BF16)
            part_ref[c] = high
            slot = candidate_slot(slots, own, c)
            acc[slot] += dot_nt(up, high) + dot_nt(up, rest)

        @pl.when(live_ref[c] == 0)
        def _():
            part_ref[c] = jnp.zeros((rows, HEAD_SIZE), BF16)

        return carried

    lax.fori_loop(0, count, second, 0)

    @pl.when(group == pl.num_programs(0) - 1)
    def _():
        proj_ref[...] = acc[...].astype(BF16)


def stats(slots, parents, lengths, key_blocks, qt, gs, up):
    count = candidate_count(slots)
    rows, width = key_blocks[0].shape
    rank = up.shape[0]
    lanes = PER * rows
    scale = LOG2E * HEAD_SIZE ** (-0.5)
    smem = pl.BlockSpec(memory_space=pltpu.SMEM)
    column = pl.BlockSpec((rows, HEAD_SIZE), lambda k: (0, k))
    return pl.pallas_call(
        functools.partial(stats_kernel, slots, scale),
        name="stats",
        grid=(KEY_HEADS,),
        out_shape=(
            jax.ShapeDtypeStruct((slots, rank, rows), BF16),
            jax.ShapeDtypeStruct((count, rows, width), BF16),
            jax.ShapeDtypeStruct((1, HQ * rows), F32),
        ),
        in_specs=[smem, smem]
        + [column] * count
        + [
            pl.BlockSpec((HEAD_SIZE, lanes), lambda k: (0, k)),
            pl.BlockSpec((lanes, HEAD_SIZE), lambda k: (k, 0)),
            pl.BlockSpec((rank, HEAD_SIZE), lambda k: (0, k)),
        ],
        out_specs=(
            pl.BlockSpec((slots, rank, rows), lambda k: (0, 0, 0)),
            pl.BlockSpec((count, rows, HEAD_SIZE), lambda k: (0, 0, k)),
            pl.BlockSpec((1, lanes), lambda k: (0, k)),
        ),
        scratch_shapes=[
            pltpu.SMEM((count,), jnp.int32),
            pltpu.VMEM((count, rows, HEAD_SIZE), BF16),
            pltpu.VMEM((count, rows, lanes), F32),
            pltpu.VMEM((count, 1, lanes), F32),
            pltpu.VMEM((slots, rank, rows), F32),
        ],
        compiler_params=pltpu.CompilerParams(vmem_limit_bytes=VMEM_LIMIT, dimension_semantics=("arbitrary",)),
        cost_estimate=pl.CostEstimate(flops=2_000_000_000, bytes_accessed=5_000_000, transcendentals=3_000_000),
    )(parents, lengths, *key_blocks, qt, gs, up)


def attend_kernel(slots, scale, inverse_root, *refs):
    count = candidate_count(slots)
    parents_ref, lengths_ref = refs[:2]
    key_refs = refs[2 : 2 + count]
    value_refs = refs[2 + count : 2 + 2 * count]
    qt_ref, gt_ref, lse_ref = refs[2 + 2 * count : 5 + 2 * count]
    attended_ref, query_grad_ref = refs[5 + 2 * count : 7 + 2 * count]
    live_ref, keys, values, weights, out_t, dq_t = refs[7 + 2 * count :]
    rows = key_refs[0].shape[0]
    own = lax.axis_index("node")

    @pl.when(pl.program_id(0) == 0)
    def _():
        mark_candidates(slots, parents_ref, lengths_ref, live_ref)

    for c in range(count):
        keys[c] = key_refs[c][...]
        values[c] = value_refs[c][...]
    key_at = lax.broadcasted_iota(jnp.int32, (rows, rows), 0)
    query_at = lax.broadcasted_iota(jnp.int32, (rows, rows), 1)
    qt = qt_ref[...]
    gt = gt_ref[...]
    lse = lse_ref[...]

    def forward(c, allowed):
        s = dot(keys[c], qt)
        s = jnp.concatenate(
            [jnp.where(allowed, s[:, i * rows : (i + 1) * rows], NEGATIVE) for i in range(PER)], axis=1
        )
        w = jnp.exp2(s * scale - lse)
        weights[c] = w
        return dot_tn(values[c], w.astype(BF16))

    out_t[...] = forward(0, (key_at <= query_at) & (key_at < live_ref[0]))

    def first(c, carried):
        @pl.when(live_ref[c] > 0)
        def _():
            out_t[...] += forward(c, key_at < live_ref[c])

        return carried

    lax.fori_loop(1, count, first, 0)
    dots = jnp.sum(gt.astype(F32) * out_t[...], axis=0, keepdims=True)
    dq_t[...] = jnp.zeros_like(dq_t)

    def second(c, carried):
        @pl.when(live_ref[c] > 0)
        def _():
            pressure = dot(values[c], gt)
            slopes = (weights[c] * (pressure - dots) * inverse_root).astype(BF16)
            dq_t[...] += dot_tn(keys[c], slopes)

        return carried

    lax.fori_loop(0, count, second, 0)
    live = lax.broadcasted_iota(jnp.int32, (rows, HEAD_SIZE), 0) < lengths_ref[0, own]
    for i in range(PER):
        cols = slice(i * HEAD_SIZE, (i + 1) * HEAD_SIZE)
        here = slice(i * rows, (i + 1) * rows)
        attended_ref[:, cols] = jnp.where(live, out_t[:, here].T, 0.0).astype(BF16)
        query_grad_ref[:, cols] = dq_t[:, here].T.astype(BF16)


def attend(slots, parents, lengths, key_blocks, value_blocks, qt, gt, lse):
    count = candidate_count(slots)
    rows = key_blocks[0].shape[0]
    lanes = PER * rows
    inverse_root = HEAD_SIZE ** (-0.5)
    smem = pl.BlockSpec(memory_space=pltpu.SMEM)
    column = pl.BlockSpec((rows, HEAD_SIZE), lambda k: (0, k))
    wide = pl.BlockSpec((HEAD_SIZE, lanes), lambda k: (0, k))
    out = pl.BlockSpec((rows, PER * HEAD_SIZE), lambda k: (0, k))
    return pl.pallas_call(
        functools.partial(attend_kernel, slots, LOG2E * inverse_root, inverse_root),
        name="attend",
        grid=(KEY_HEADS,),
        out_shape=(jax.ShapeDtypeStruct((rows, HQ * HEAD_SIZE), BF16),) * 2,
        in_specs=[smem, smem] + [column] * (2 * count) + [wide, wide, pl.BlockSpec((1, lanes), lambda k: (0, k))],
        out_specs=(out, out),
        scratch_shapes=[
            pltpu.SMEM((count,), jnp.int32),
            pltpu.VMEM((count, rows, HEAD_SIZE), BF16),
            pltpu.VMEM((count, rows, HEAD_SIZE), BF16),
            pltpu.VMEM((count, rows, lanes), F32),
            pltpu.VMEM((HEAD_SIZE, lanes), F32),
            pltpu.VMEM((HEAD_SIZE, lanes), F32),
        ],
        compiler_params=pltpu.CompilerParams(vmem_limit_bytes=VMEM_LIMIT, dimension_semantics=("arbitrary",)),
        cost_estimate=pl.CostEstimate(flops=3_000_000_000, bytes_accessed=5_000_000, transcendentals=3_000_000),
    )(parents, lengths, *key_blocks, *value_blocks, qt, gt, lse)


def gradient_kernel(factor, *refs):
    received_ref, x_ref, part_ref = refs[:3]
    message_refs = refs[3:-2]
    keep_ref, send_ref = refs[-2:]
    rows, width = x_ref.shape
    rank = received_ref.shape[1]
    inner = part_ref.shape[2]
    core = lax.axis_index("rep")
    half = keep_ref.shape[1]
    total = jnp.sum(received_ref[...].astype(F32), axis=0).astype(BF16)
    up = None
    for c, message_ref in enumerate(message_refs):
        low_t = jnp.concatenate([message_ref[:, :rows], message_ref[:, rows : 2 * rows]], axis=0)
        term = dot(low_t, part_ref[c])
        up = term if up is None else up + term

    def half_of(which):
        if which == 0:
            return dot(total, x_ref[:, :half]) * factor
        down = dot(total, x_ref[:, half:]) * factor
        return jnp.concatenate([down, up * factor], axis=1)

    for mine in range(2):

        @pl.when(core == mine)
        def _():
            keep_ref[...] = half_of(mine)
            send_ref[...] = half_of(1 - mine).astype(BF16)


def gradients(received, x, parts, messages, factor):
    rows, width = x.shape
    count, _, inner = parts.shape
    rank = received.shape[1]
    half = (width + inner) // 2
    vm = pl.BlockSpec(memory_space=pltpu.VMEM)
    extra = rank // 2
    low = pl.BlockSpec((extra, inner), lambda i: (rows // extra, 0))
    return pl.pallas_call(
        functools.partial(gradient_kernel, factor),
        name="gradients",
        grid=(1,),
        out_shape=(
            jax.ShapeDtypeStruct((rank, half), F32),
            jax.ShapeDtypeStruct((rank, half), BF16),
        ),
        in_specs=[vm] * 3 + [low] * count,
        out_specs=(vm, vm),
        compiler_params=pltpu.CompilerParams(vmem_limit_bytes=VMEM_LIMIT),
        cost_estimate=pl.CostEstimate(flops=80_000_000, bytes_accessed=4_000_000, transcendentals=0),
    )(received, x, parts, *messages)


def gather_blocks(slots, block):
    if not paired(slots):
        own = lax.axis_index("node")
        whole = lax.all_gather(block, "node")
        return [block] + [
            lax.dynamic_index_in_dim(whole, jnp.maximum(candidate_slot(slots, own, c), 0), 0, keepdims=False)
            for c in range(1, candidate_count(slots))
        ]
    swap = [(i, i ^ 1) for i in range(slots)]
    columns = [block] + [
        lax.ppermute(block, "node", [(i, i + d) for i in range(slots - d)]) for d in range(2, slots, 2)
    ]
    blocks = []
    for column in columns:
        blocks += [column, lax.ppermute(column, "node", swap)]
    return blocks


def sum_over_all(slots, keep, send):
    core = lax.axis_index("rep")
    own = lax.axis_index("node")
    swap_core = [(0, 1), (1, 0)]

    def swap(x, bit):
        return lax.ppermute(x, "node", [(i, i ^ bit) for i in range(slots)])

    total = keep + lax.ppermute(send, "rep", swap_core).astype(F32)
    quarter = total.shape[1] // 2
    low, high = total[:, :quarter], total[:, quarter:]
    odd = own % 2 == 1
    mine = jnp.where(odd, high, low)
    other = jnp.where(odd, low, high).astype(BF16)
    mine = (mine + swap(other, 1).astype(F32)).astype(BF16)
    bit = 2
    while bit < slots:
        mine = (mine.astype(F32) + swap(mine, bit).astype(F32)).astype(BF16)
        bit *= 2
    other = swap(mine, 1)
    half = jnp.concatenate([jnp.where(odd, other, mine), jnp.where(odd, mine, other)], axis=1)
    other = lax.ppermute(half, "rep", swap_core)
    second = core == 1
    whole = jnp.concatenate([jnp.where(second, other, half), jnp.where(second, half, other)], axis=1)
    return whole.astype(F32)


def on_device(
    normed_input,
    queries,
    rotated_key_heads,
    frozen_value_rows,
    adapter_down_weight,
    adapter_up_weight,
    output_gradient,
    parents,
    lengths,
):
    x = normed_input[0]
    rows, width = x.shape
    slots = lax.axis_size("node")
    key_blocks = gather_blocks(slots, rotated_key_heads[0])
    message, qt, gt, gs = prepare(
        lengths, x, adapter_down_weight.T, adapter_up_weight, frozen_value_rows[0], queries[0], output_gradient[0]
    )
    messages = gather_blocks(slots, message)
    projected, parts, lse = stats(slots, parents, lengths, key_blocks, qt, gs, adapter_up_weight)
    received = lax.all_to_all(projected, "node", 0, 0)
    factor = (slots * lax.axis_size("rep") * rows) ** (-0.5)
    keep, send = gradients(received, x, parts, messages, factor)
    whole = sum_over_all(slots, keep, send)
    attended, query_grad = attend(slots, parents, lengths, key_blocks, messages, qt, gt, lse)
    return (attended[None], query_grad[None], whole[:, :width].T, whole[:, width:])


def solution(mesh):
    tokens = P(("groups", "rep"), "node", None)
    trees = P(("groups", "rep"), None)
    return jax.shard_map(
        on_device,
        mesh=mesh,
        in_specs=(tokens,) * 4 + (P(), P()) + (tokens, trees, trees),
        out_specs=(tokens, tokens, P("groups", None), P("groups", None)),
        check_vma=False,
    )
```

```python
import functools

import jax
import jax.numpy as jnp
from jax import lax
from jax.experimental import pallas as pl
from jax.experimental.pallas import tpu as pltpu
from jax.sharding import PartitionSpec as P


HQ = 20
KEY_HEADS = 4
HEAD_SIZE = 128
PROMPT = 2
SPAN = 5
PER = HQ // KEY_HEADS

NEGATIVE = -1e30
LOG2E = 1.4426950408889634
F32 = jnp.float32
BF16 = jnp.bfloat16


VMEM_LIMIT = 56 * 1024 * 1024


def dot(a, b):
    return lax.dot_general(a, b, (((1,), (0,)), ((), ())), preferred_element_type=F32)


def dot_nt(a, b):
    return lax.dot_general(a, b, (((1,), (1,)), ((), ())), preferred_element_type=F32)


def dot_tn(a, b):
    return lax.dot_general(a, b, (((0,), (0,)), ((), ())), preferred_element_type=F32)


def paired(slots):
    return slots % 2 == 0 and slots <= 1 + PROMPT + SPAN


def candidate_count(slots):
    return slots if paired(slots) else 1 + PROMPT + SPAN


def candidate_slot(slots, own, c):
    if paired(slots):
        pair = own - (c // 2) * 2
        slot = pair + (c % 2) * (1 - 2 * (pair % 2))
        return jnp.where(pair >= 0, slot, -1)
    window = own - c
    window = jnp.where(window >= PROMPT, window, -1)
    prompt = c - SPAN - 1
    prompt = jnp.where(prompt < own, prompt, -1)
    return jnp.where(c == 0, own, jnp.where(c <= SPAN, window, prompt))


def mark_candidates(slots, parents_ref, lengths_ref, live_ref):
    own = lax.axis_index("node")
    count = candidate_count(slots)
    for c in range(count):
        live_ref[c] = 0
    live_ref[0] = lengths_ref[0, own]

    def climb(step, current):
        at = jnp.maximum(current, 0)
        for c in range(1, count):
            slot = candidate_slot(slots, own, c)

            @pl.when((slot == current) & (current >= 0))
            def _():
                live_ref[c] = lengths_ref[0, at]

        return jnp.where(current >= 0, parents_ref[0, at], -1)

    lax.fori_loop(0, PROMPT + SPAN, climb, parents_ref[0, own])


def prepare_kernel(
    lengths_ref, x_ref, down_ref, up_ref, frozen_ref, q_ref, g_ref,
    message_ref, qt_ref, gt_ref, gs_ref,
):
    own = lax.axis_index("node")
    rows = x_ref.shape[0]
    width = frozen_ref.shape[1]
    low_t = dot_nt(down_ref[...], x_ref[...]).astype(BF16)
    values = frozen_ref[...].astype(F32) + dot_tn(low_t, up_ref[...])
    message_ref[:rows, :] = values.astype(BF16)
    half = low_t.shape[0] // 2
    message_ref[rows:, :] = jnp.zeros((half, width), BF16)
    message_ref[rows:, :rows] = low_t[:half]
    message_ref[rows:, rows : 2 * rows] = low_t[half:]
    length = lengths_ref[0, own]
    live = lax.broadcasted_iota(jnp.int32, (rows, HEAD_SIZE), 0) < length
    for h in range(HQ):
        cols = slice(h * HEAD_SIZE, (h + 1) * HEAD_SIZE)
        here = slice(h * rows, (h + 1) * rows)
        qt_ref[:, here] = q_ref[:, cols].T
        g = jnp.where(live, g_ref[:, cols].astype(F32), 0.0).astype(BF16)
        gs_ref[here, :] = g
        gt_ref[:, here] = g.T


def prepare(lengths, x, down_t, up, frozen, q, g):
    rows = x.shape[0]
    rank, width = up.shape
    vm = pl.BlockSpec(memory_space=pltpu.VMEM)
    return pl.pallas_call(
        prepare_kernel,
        name="prepare",
        out_shape=(
            jax.ShapeDtypeStruct((rows + rank // 2, width), BF16),
            jax.ShapeDtypeStruct((HEAD_SIZE, HQ * rows), BF16),
            jax.ShapeDtypeStruct((HEAD_SIZE, HQ * rows), BF16),
            jax.ShapeDtypeStruct((HQ * rows, HEAD_SIZE), BF16),
        ),
        in_specs=[pl.BlockSpec(memory_space=pltpu.SMEM)] + [vm] * 6,
        out_specs=(vm,) * 4,
        compiler_params=pltpu.CompilerParams(vmem_limit_bytes=VMEM_LIMIT),
        cost_estimate=pl.CostEstimate(flops=100_000_000, bytes_accessed=6_000_000, transcendentals=0),
    )(lengths, x, down_t, up, frozen, q, g)


def fill_bias(live_ref, bias_ref):
    rows = bias_ref.shape[1]
    key_at = lax.broadcasted_iota(jnp.int32, (rows, rows), 0)
    query_at = lax.broadcasted_iota(jnp.int32, (rows, rows), 1)
    for c in range(live_ref.shape[0]):
        allowed = key_at < live_ref[c]
        if c == 0:
            allowed &= key_at <= query_at
        bias_ref[c] = jnp.where(allowed, 0.0, NEGATIVE)


def stats_kernel(slots, scale, *refs):
    count = candidate_count(slots)
    parents_ref, lengths_ref = refs[:2]
    key_refs = refs[2 : 2 + count]
    qt_ref, gs_ref, up_ref = refs[2 + count : 5 + count]
    proj_ref, part_ref, lse_ref = refs[5 + count : 8 + count]
    live_ref, keys, weights, bias, tops, acc = refs[8 + count :]
    group = pl.program_id(0)
    rows = key_refs[0].shape[0]
    own = lax.axis_index("node")

    @pl.when(group == 0)
    def _():
        mark_candidates(slots, parents_ref, lengths_ref, live_ref)
        fill_bias(live_ref, bias)
        acc[...] = jnp.zeros_like(acc)

    for c in range(count):
        keys[c * rows : (c + 1) * rows] = key_refs[c][...]
    top = [None] * PER
    total = [None] * PER
    for j in range(0, count, 2):
        pair = slice(j * rows, (j + 2) * rows)
        for h in range(PER):
            here = slice(h * rows, (h + 1) * rows)
            s = dot(keys[pair], qt_ref[:, here])
            s = jnp.concatenate([s[:rows] + bias[j], s[rows:] + bias[j + 1]], axis=0)
            high = jnp.max(s, axis=0, keepdims=True) * scale
            raised = high if j == 0 else jnp.maximum(top[h], high)
            p = jnp.exp2(s * scale - raised)
            weights[pair, here] = p
            tops[j // 2 : j // 2 + 1, here] = raised
            summed = jnp.sum(p, axis=0, keepdims=True)
            total[h] = summed if j == 0 else total[h] * jnp.exp2(top[h] - raised) + summed
            top[h] = raised
    for h in range(PER):
        here = slice(h * rows, (h + 1) * rows)
        lse_ref[:, here] = top[h] + jnp.log2(total[h])
    inverse = [1.0 / total[h] for h in range(PER)]
    up = up_ref[...]
    gs = gs_ref[...]
    for j in range(0, count, 2):
        pair = slice(j * rows, (j + 2) * rows)
        scaled = []
        for h in range(PER):
            here = slice(h * rows, (h + 1) * rows)
            factor = jnp.exp2(tops[j // 2 : j // 2 + 1, here] - top[h]) * inverse[h]
            scaled.append((weights[pair, here] * factor).astype(BF16))
        part = dot(jnp.concatenate(scaled, axis=1), gs)
        high = part.astype(BF16)
        rest = (part - high.astype(F32)).astype(BF16)
        proj = dot_nt(up, high) + dot_nt(up, rest)
        for c in (j, j + 1):
            half = slice((c - j) * rows, (c - j + 1) * rows)
            part_ref[c] = high[half]
            acc[c] += proj[:, half]

    @pl.when(group == pl.num_programs(0) - 1)
    def _():
        proj_ref[...] = jnp.zeros_like(proj_ref)
        for c in range(count):

            @pl.when(live_ref[c] > 0)
            def _():
                proj_ref[candidate_slot(slots, own, c)] = acc[c]


def stats(slots, parents, lengths, key_blocks, qt, gs, up):
    count = candidate_count(slots)
    rows, width = key_blocks[0].shape
    rank = up.shape[0]
    lanes = PER * rows
    scale = LOG2E * HEAD_SIZE ** (-0.5)
    smem = pl.BlockSpec(memory_space=pltpu.SMEM)
    column = pl.BlockSpec((rows, HEAD_SIZE), lambda k: (0, k))
    return pl.pallas_call(
        functools.partial(stats_kernel, slots, scale),
        name="stats",
        grid=(KEY_HEADS,),
        out_shape=(
            jax.ShapeDtypeStruct((slots, rank, rows), F32),
            jax.ShapeDtypeStruct((count, rows, width), BF16),
            jax.ShapeDtypeStruct((1, HQ * rows), F32),
        ),
        in_specs=[smem, smem]
        + [column] * count
        + [
            pl.BlockSpec((HEAD_SIZE, lanes), lambda k: (0, k)),
            pl.BlockSpec((lanes, HEAD_SIZE), lambda k: (k, 0)),
            pl.BlockSpec((rank, HEAD_SIZE), lambda k: (0, k)),
        ],
        out_specs=(
            pl.BlockSpec((slots, rank, rows), lambda k: (0, 0, 0)),
            pl.BlockSpec((count, rows, HEAD_SIZE), lambda k: (0, 0, k)),
            pl.BlockSpec((1, lanes), lambda k: (0, k)),
        ),
        scratch_shapes=[
            pltpu.SMEM((count,), jnp.int32),
            pltpu.VMEM((count * rows, HEAD_SIZE), BF16),
            pltpu.VMEM((count * rows, lanes), F32),
            pltpu.VMEM((count, rows, rows), F32),
            pltpu.VMEM((8, lanes), F32),
            pltpu.VMEM((count, rank, rows), F32),
        ],
        compiler_params=pltpu.CompilerParams(vmem_limit_bytes=VMEM_LIMIT, dimension_semantics=("arbitrary",)),
        cost_estimate=pl.CostEstimate(flops=2_000_000_000, bytes_accessed=5_000_000, transcendentals=3_000_000),
    )(parents, lengths, *key_blocks, qt, gs, up)


def attend_kernel(slots, scale, inverse_root, *refs):
    count = candidate_count(slots)
    parents_ref, lengths_ref = refs[:2]
    key_refs = refs[2 : 2 + count]
    value_refs = refs[2 + count : 2 + 2 * count]
    qt_ref, gt_ref, lse_ref = refs[2 + 2 * count : 5 + 2 * count]
    attended_ref, query_grad_ref = refs[-10:-8]
    live_ref, keys, values, weights, rounded, slopes, bias, out_t = refs[-8:]
    rows = key_refs[0].shape[0]
    own = lax.axis_index("node")
    mark_candidates(slots, parents_ref, lengths_ref, live_ref)
    fill_bias(live_ref, bias)
    for c in range(count):
        block = slice(c * rows, (c + 1) * rows)
        keys[block] = key_refs[c][...]
        values[block] = value_refs[c][...]
    for j in range(0, count, 2):
        pair = slice(j * rows, (j + 2) * rows)
        for h in range(PER):
            here = slice(h * rows, (h + 1) * rows)
            s = dot(keys[pair], qt_ref[:, here])
            s = jnp.concatenate([s[:rows] + bias[j], s[rows:] + bias[j + 1]], axis=0)
            w = jnp.exp2(s * scale - lse_ref[:, here])
            weights[pair, here] = w
            rounded[pair, here] = w.astype(BF16)
    values_t = values[...].T
    keys_t = keys[...].T
    dots = []
    for h in range(PER):
        here = slice(h * rows, (h + 1) * rows)
        out = dot(values_t, rounded[:, here])
        out_t[:, here] = out
        dots.append(jnp.sum(gt_ref[:, here].astype(F32) * out, axis=0, keepdims=True))
    for j in range(0, count, 2):
        pair = slice(j * rows, (j + 2) * rows)
        for h in range(PER):
            here = slice(h * rows, (h + 1) * rows)
            pressure = dot(values[pair], gt_ref[:, here])
            slopes[pair, here] = (weights[pair, here] * (pressure - dots[h]) * inverse_root).astype(BF16)
    live = lax.broadcasted_iota(jnp.int32, (rows, HEAD_SIZE), 0) < lengths_ref[0, own]
    for h in range(PER):
        cols = slice(h * HEAD_SIZE, (h + 1) * HEAD_SIZE)
        here = slice(h * rows, (h + 1) * rows)
        query_grad_ref[:, cols] = dot(keys_t, slopes[:, here]).T.astype(BF16)
        attended_ref[:, cols] = jnp.where(live, out_t[:, here].T, 0.0).astype(BF16)


def attend(slots, group, carried, parents, lengths, key_blocks, value_blocks, qt, gt, lse):
    count = candidate_count(slots)
    rows = key_blocks[0].shape[0]
    lanes = PER * rows
    inverse_root = HEAD_SIZE ** (-0.5)
    smem = pl.BlockSpec(memory_space=pltpu.SMEM)
    column = pl.BlockSpec((rows, HEAD_SIZE), lambda i: (0, group))
    wide = pl.BlockSpec((HEAD_SIZE, lanes), lambda i: (0, group))
    out = pl.BlockSpec((rows, PER * HEAD_SIZE), lambda i: (0, group))
    first = 5 + 2 * count
    return pl.pallas_call(
        functools.partial(attend_kernel, slots, LOG2E * inverse_root, inverse_root),
        name="attend",
        grid=(1,),
        out_shape=(jax.ShapeDtypeStruct((rows, HQ * HEAD_SIZE), BF16),) * 2,
        in_specs=[smem, smem]
        + [column] * (2 * count)
        + [wide, wide, pl.BlockSpec((1, lanes), lambda i: (0, group))]
        + [pl.BlockSpec(memory_space=pl.ANY)] * len(carried),
        out_specs=(out, out),
        scratch_shapes=[
            pltpu.SMEM((count,), jnp.int32),
            pltpu.VMEM((count * rows, HEAD_SIZE), BF16),
            pltpu.VMEM((count * rows, HEAD_SIZE), BF16),
            pltpu.VMEM((count * rows, lanes), F32),
            pltpu.VMEM((count * rows, lanes), BF16),
            pltpu.VMEM((count * rows, lanes), BF16),
            pltpu.VMEM((count, rows, rows), F32),
            pltpu.VMEM((HEAD_SIZE, lanes), F32),
        ],
        input_output_aliases={first + i: i for i in range(len(carried))},
        compiler_params=pltpu.CompilerParams(vmem_limit_bytes=VMEM_LIMIT, dimension_semantics=("arbitrary",)),
        cost_estimate=pl.CostEstimate(flops=800_000_000, bytes_accessed=1_500_000, transcendentals=700_000),
    )(parents, lengths, *key_blocks, *value_blocks, qt, gt, lse, *carried)


def gradient_kernel(factor, received_ref, x_ref, part_ref, even_ref, odd_ref, keep_ref, send_ref):
    rows, width = x_ref.shape
    rank = received_ref.shape[1]
    core = lax.axis_index("rep")
    half = keep_ref.shape[1]
    start = width - half
    total = jnp.sum(received_ref[...], axis=0).astype(BF16)

    def place(ref, which):
        if which == 0:
            ref[...] = dot(total, x_ref[:, :half]) * factor
        else:
            ref[:, :start] = dot(total, x_ref[:, half:]) * factor

    for mine in range(2):

        @pl.when(core == mine)
        def _():
            place(send_ref, 1 - mine)
            place(keep_ref, mine)

    up = None
    for c in range(part_ref.shape[0]):
        slab = (odd_ref if c % 2 else even_ref)[(c // 2) * (rank // 2) : (c // 2 + 1) * (rank // 2), : 2 * rows]
        term = dot(jnp.concatenate([slab[:, :rows], slab[:, rows:]], axis=0), part_ref[c])
        up = term if up is None else up + term
    up = up * factor

    @pl.when(core == 0)
    def _():
        send_ref[:, start:] = up

    @pl.when(core == 1)
    def _():
        keep_ref[:, start:] = up


def gradients(received, x, parts, even, odd, factor):
    _, width = x.shape
    inner = parts.shape[2]
    rank = received.shape[1]
    half = (width + inner) // 2
    vm = pl.BlockSpec(memory_space=pltpu.VMEM)
    return pl.pallas_call(
        functools.partial(gradient_kernel, factor),
        name="gradients",
        out_shape=(jax.ShapeDtypeStruct((rank, half), F32),) * 2,
        in_specs=[vm] * 5,
        out_specs=(vm, vm),
        compiler_params=pltpu.CompilerParams(vmem_limit_bytes=VMEM_LIMIT),
        cost_estimate=pl.CostEstimate(flops=80_000_000, bytes_accessed=4_000_000, transcendentals=0),
    )(received, x, parts, even, odd)


def gather_blocks(slots, block):
    if not paired(slots):
        own = lax.axis_index("node")
        whole = lax.all_gather(block, "node")
        return [block] + [
            lax.dynamic_index_in_dim(whole, jnp.maximum(candidate_slot(slots, own, c), 0), 0, keepdims=False)
            for c in range(1, candidate_count(slots))
        ]
    swap = [(i, i ^ 1) for i in range(slots)]
    columns = [block]
    for d in range(2, slots, 2):
        columns.append(lax.ppermute(block, "node", [(i, i + d) for i in range(slots - d)]))
    blocks = []
    for column in columns:
        blocks += [column, lax.ppermute(column, "node", swap)]
    return blocks


def sum_over_all(slots, keep, send):
    core = lax.axis_index("rep")
    own = lax.axis_index("node")
    swap_core = [(0, 1), (1, 0)]

    def swap(x, bit):
        return lax.ppermute(x, "node", [(i, i ^ bit) for i in range(slots)])

    came = lax.ppermute(send, "rep", swap_core)
    total = keep + came
    quarter = total.shape[1] // 2
    low, high = total[:, :quarter], total[:, quarter:]
    odd = own % 2 == 1
    mine = jnp.where(odd, high, low)
    other = jnp.where(odd, low, high).astype(BF16)
    mine = (mine + swap(other, 1).astype(F32)).astype(BF16)
    bit = 2
    while bit < slots:
        mine = (mine.astype(F32) + swap(mine, bit).astype(F32)).astype(BF16)
        bit *= 2
    other = swap(mine, 1)
    half = jnp.concatenate([jnp.where(odd, other, mine), jnp.where(odd, mine, other)], axis=1)
    other = lax.ppermute(half, "rep", swap_core)
    second = core == 1
    whole = jnp.concatenate([jnp.where(second, other, half), jnp.where(second, half, other)], axis=1)
    return whole.astype(F32)


def on_device(
    normed_input,
    queries,
    rotated_key_heads,
    frozen_value_rows,
    adapter_down_weight,
    adapter_up_weight,
    output_gradient,
    parents,
    lengths,
):
    x = normed_input[0]
    rows, width = x.shape
    slots = lax.axis_size("node")
    key_blocks = gather_blocks(slots, rotated_key_heads[0])
    message, qt, gt, gs = prepare(
        lengths, x, adapter_down_weight.T, adapter_up_weight, frozen_value_rows[0], queries[0], output_gradient[0]
    )
    messages = gather_blocks(slots, message)
    projected, parts, lse = stats(slots, parents, lengths, key_blocks, qt, gs, adapter_up_weight)
    received = lax.all_to_all(projected, "node", 0, 0)
    factor = (slots * lax.axis_size("rep") * rows) ** (-0.5)
    slabs = [message[rows:] for message in messages]
    even = jnp.concatenate(slabs[0::2], axis=0)
    if paired(slots):
        odd = lax.ppermute(even, "node", [(i, i ^ 1) for i in range(slots)])
    else:
        odd = jnp.concatenate(slabs[1::2], axis=0)
    keep, send = gradients(received, x, parts, even, odd, factor)
    whole = sum_over_all(slots, keep, send)
    carried = ()
    for group in range(KEY_HEADS):
        carried = attend(slots, group, carried, parents, lengths, key_blocks, messages, qt, gt, lse)
    attended, query_grad = carried
    return (attended[None], query_grad[None], whole[:, :width].T, whole[:, width:])


def solution(mesh):
    tokens = P(("groups", "rep"), "node", None)
    trees = P(("groups", "rep"), None)
    return jax.shard_map(
        on_device,
        mesh=mesh,
        in_specs=(tokens,) * 4 + (P(), P()) + (tokens, trees, trees),
        out_specs=(tokens, tokens, P("groups", None), P("groups", None)),
        check_vma=False,
    )
```

```python
import functools

import jax
import jax.numpy as jnp
from jax import lax
from jax.experimental import pallas as pl
from jax.experimental.pallas import tpu as pltpu
from jax.sharding import PartitionSpec as P


HQ = 20
KEY_HEADS = 4
HEAD_SIZE = 128
PROMPT = 2
SPAN = 5
PER = HQ // KEY_HEADS

NEGATIVE = -1e30
LOG2E = 1.4426950408889634
F32 = jnp.float32
BF16 = jnp.bfloat16


VMEM_LIMIT = 56 * 1024 * 1024
SMALL_LIMIT = 16 * 1024 * 1024


def dot(a, b):
    return lax.dot_general(a, b, (((1,), (0,)), ((), ())), preferred_element_type=F32)


def dot_nt(a, b):
    return lax.dot_general(a, b, (((1,), (1,)), ((), ())), preferred_element_type=F32)


def dot_tn(a, b):
    return lax.dot_general(a, b, (((0,), (0,)), ((), ())), preferred_element_type=F32)


def paired(slots):
    return slots % 2 == 0 and slots <= 1 + PROMPT + SPAN


def candidate_count(slots):
    return slots if paired(slots) else 1 + PROMPT + SPAN


def candidate_slot(slots, own, c):
    if paired(slots):
        pair = own - (c // 2) * 2
        slot = pair + (c % 2) * (1 - 2 * (pair % 2))
        return jnp.where(pair >= 0, slot, -1)
    window = own - c
    window = jnp.where(window >= PROMPT, window, -1)
    prompt = c - SPAN - 1
    prompt = jnp.where(prompt < own, prompt, -1)
    return jnp.where(c == 0, own, jnp.where(c <= SPAN, window, prompt))


def value_index(slots, own, j):
    return jnp.maximum(own // 2 - j, 0) if paired(slots) else j


def mark_candidates(slots, parents_ref, lengths_ref, live_ref):
    own = lax.axis_index("node")
    count = candidate_count(slots)
    for c in range(count):
        live_ref[c] = 0
    live_ref[0] = lengths_ref[0, own]

    def climb(step, current):
        at = jnp.maximum(current, 0)
        for c in range(1, count):
            slot = candidate_slot(slots, own, c)

            @pl.when((slot == current) & (current >= 0))
            def _():
                live_ref[c] = lengths_ref[0, at]

        return jnp.where(current >= 0, parents_ref[0, at], -1)

    lax.fori_loop(0, PROMPT + SPAN, climb, parents_ref[0, own])


def prepare_kernel(
    lengths_ref, x_ref, down_ref, up_ref, frozen_ref, q_ref, g_ref,
    message_ref, low_ref, qt_ref, gt_ref,
):
    own = lax.axis_index("node")
    rows = x_ref.shape[0]
    low_t = dot_nt(down_ref[...], x_ref[...]).astype(BF16)
    values = frozen_ref[...].astype(F32) + dot_tn(low_t, up_ref[...])
    low_ref[...] = low_t
    for i in range(message_ref.shape[0]):
        message_ref[i] = values.astype(BF16)
    length = lengths_ref[0, own]
    live = lax.broadcasted_iota(jnp.int32, (rows, HEAD_SIZE), 0) < length
    for h in range(HQ):
        cols = slice(h * HEAD_SIZE, (h + 1) * HEAD_SIZE)
        here = slice(h * rows, (h + 1) * rows)
        qt_ref[:, here] = q_ref[:, cols].T
        g = jnp.where(live, g_ref[:, cols].astype(F32), 0.0).astype(BF16)
        gt_ref[:, here] = g.T


def prepare(copies, lengths, x, down_t, up, frozen, q, g):
    rows = x.shape[0]
    rank, width = up.shape
    vm = pl.BlockSpec(memory_space=pltpu.VMEM)
    return pl.pallas_call(
        prepare_kernel,
        name="prepare",
        out_shape=(
            jax.ShapeDtypeStruct((copies, rows, width), BF16),
            jax.ShapeDtypeStruct((rank, rows), BF16),
            jax.ShapeDtypeStruct((HEAD_SIZE, HQ * rows), BF16),
            jax.ShapeDtypeStruct((HEAD_SIZE, HQ * rows), BF16),
        ),
        in_specs=[pl.BlockSpec(memory_space=pltpu.SMEM)] + [vm] * 6,
        out_specs=(vm,) * 4,
        compiler_params=pltpu.CompilerParams(vmem_limit_bytes=VMEM_LIMIT),
        cost_estimate=pl.CostEstimate(flops=100_000_000, bytes_accessed=6_000_000, transcendentals=0),
    )(lengths, x, down_t, up, frozen, q, g)


def fill_masks(live_ref, mask_ref, causal_ref):
    rows = causal_ref.shape[0]
    key_at = lax.broadcasted_iota(jnp.int32, (rows, rows), 0)
    across = lax.broadcasted_iota(jnp.int32, (rows, rows), 1)
    for c in range(live_ref.shape[0]):
        dead = (across == 0) & (key_at >= live_ref[c])
        mask_ref[c * rows : (c + 1) * rows] = jnp.where(dead, NEGATIVE, 0.0).astype(BF16)
    causal_ref[...] = jnp.where(key_at <= across, 0.0, NEGATIVE)


def first_row(rows, lanes):
    return jnp.where(lax.broadcasted_iota(jnp.int32, (rows, lanes), 0) == 0, 1.0, 0.0).astype(BF16)


def fill_bias(live_ref, bias_ref):
    rows = bias_ref.shape[1]
    key_at = lax.broadcasted_iota(jnp.int32, (rows, rows), 0)
    query_at = lax.broadcasted_iota(jnp.int32, (rows, rows), 1)
    for c in range(live_ref.shape[0]):
        allowed = key_at < live_ref[c]
        if c == 0:
            allowed &= key_at <= query_at
        bias_ref[c] = jnp.where(allowed, 0.0, NEGATIVE)


def fold(x, op):
    return op(x.reshape(x.shape[0] // 8, 8, x.shape[1]), axis=0)


def stats_kernel(slots, scale, *refs):
    count = candidate_count(slots)
    parents_ref, lengths_ref = refs[:2]
    key_refs = refs[2 : 2 + count]
    qt_ref, gt_ref, up_ref, low_ref = refs[2 + count : 6 + count]
    proj_ref, part_ref, lse_ref = refs[6 + count : 9 + count]
    live_ref, keys, weights, bias, scores, shares, rest = refs[9 + count :]
    rows = key_refs[0].shape[0]
    own = lax.axis_index("node")
    mark_candidates(slots, parents_ref, lengths_ref, live_ref)
    fill_bias(live_ref, bias)
    for c in range(count):
        keys[c * rows : (c + 1) * rows] = key_refs[c][...]

    def lanes_of(h):
        return pl.ds(pl.multiple_of(h * rows, rows), rows)

    def step(it, carried):
        top, inverse = carried
        here = jnp.minimum(it, HQ - 1)
        before = jnp.clip(it - 1, 0, HQ - 1)
        last = jnp.maximum(it - 2, 0)
        columns = pl.ds(pl.multiple_of((here // PER) * HEAD_SIZE, HEAD_SIZE), HEAD_SIZE)
        q = qt_ref[:, lanes_of(here)]
        high = summed = None
        fresh = dot(keys[:, columns], q)
        for c in range(count):
            block = slice(c * rows, (c + 1) * rows)
            weights[block, lanes_of(last)] = (shares[block] * inverse).astype(BF16)
            p = jnp.exp2(scores[block] * scale - top)
            shares[block] = p
            part = fold(p, jnp.sum)
            summed = part if c == 0 else summed + part
            s = fresh[block] + bias[c]
            scores[block] = s
            most = fold(s, jnp.max)
            high = most if c == 0 else jnp.maximum(high, most)
        total = jnp.sum(summed, axis=0, keepdims=True)
        lse_ref[:, lanes_of(before)] = top + jnp.log2(total)
        return jnp.max(high, axis=0, keepdims=True) * scale, 1.0 / total

    empty = jnp.zeros((1, rows), F32)
    lax.fori_loop(0, HQ + 2, step, (empty, empty), unroll=2)
    for k in range(KEY_HEADS):
        lanes = slice(k * PER * rows, (k + 1) * PER * rows)
        cols = slice(k * HEAD_SIZE, (k + 1) * HEAD_SIZE)
        part = dot_nt(gt_ref[:, lanes], weights[:, lanes])
        high = part.astype(BF16)
        part_ref[cols] = high
        rest[cols] = (part - high.astype(F32)).astype(BF16)
    up = up_ref[...]
    proj = dot(up, part_ref[...]) + dot(up, rest[...])
    low = low_ref[...].astype(F32)
    for slot in range(slots):
        proj_ref[slot] = jnp.where(slot > own, low, 0.0)
    for c in range(count):

        @pl.when(live_ref[c] > 0)
        def _():
            proj_ref[candidate_slot(slots, own, c)] = proj[:, c * rows : (c + 1) * rows]


def stats(slots, parents, lengths, key_blocks, qt, gt, up, low):
    count = candidate_count(slots)
    rows, width = key_blocks[0].shape
    rank = up.shape[0]
    scale = LOG2E * HEAD_SIZE ** (-0.5)
    smem = pl.BlockSpec(memory_space=pltpu.SMEM)
    vm = pl.BlockSpec(memory_space=pltpu.VMEM)
    return pl.pallas_call(
        functools.partial(stats_kernel, slots, scale),
        name="stats",
        out_shape=(
            jax.ShapeDtypeStruct((slots, rank, rows), F32),
            jax.ShapeDtypeStruct((width, count * rows), BF16),
            jax.ShapeDtypeStruct((1, HQ * rows), F32),
        ),
        in_specs=[smem, smem] + [vm] * (count + 4),
        out_specs=(vm, vm, vm),
        scratch_shapes=[
            pltpu.SMEM((count,), jnp.int32),
            pltpu.VMEM((count * rows, width), BF16),
            pltpu.VMEM((count * rows, HQ * rows), BF16),
            pltpu.VMEM((count, rows, rows), F32),
            pltpu.VMEM((count * rows, rows), F32),
            pltpu.VMEM((count * rows, rows), F32),
            pltpu.VMEM((width, count * rows), BF16),
        ],
        compiler_params=pltpu.CompilerParams(vmem_limit_bytes=VMEM_LIMIT),
        cost_estimate=pl.CostEstimate(flops=2_000_000_000, bytes_accessed=5_000_000, transcendentals=3_000_000),
    )(parents, lengths, *key_blocks, qt, gt, up, low)


def attend_kernel(slots, group, scale, inverse_root, *refs):
    count = candidate_count(slots)
    parents_ref, lengths_ref = refs[:2]
    key_refs = refs[2 : 2 + count]
    value_refs = refs[2 + count : 4 + count]
    qt_ref, gt_ref, lse_ref = refs[4 + count : 7 + count]
    outs = refs[-13:-11]
    live_ref, keys, values, weights, rounded, slopes, masks, causal, out_t, done, sems = refs[-11:]
    rows = key_refs[0].shape[0]
    head = slice(group * HEAD_SIZE, (group + 1) * HEAD_SIZE)
    qt_ref, gt_ref, lse_ref = (
        ref.at[:, group * PER * rows : (group + 1) * PER * rows] for ref in (qt_ref, gt_ref, lse_ref)
    )
    own = lax.axis_index("node")
    mark_candidates(slots, parents_ref, lengths_ref, live_ref)
    fill_masks(live_ref, masks, causal)
    ones = first_row(HEAD_SIZE, rows)
    for c in range(count):
        block = slice(c * rows, (c + 1) * rows)
        keys[block] = key_refs[c][:, head]
        values[block] = value_refs[c % 2][value_index(slots, own, c // 2), :, head]
    for h in range(PER):
        here = slice(h * rows, (h + 1) * rows)
        s = dot(
            jnp.concatenate([keys[...], masks[...]], axis=1), jnp.concatenate([qt_ref[:, here], ones], axis=0)
        )
        for c in range(count):
            block = slice(c * rows, (c + 1) * rows)
            t = s[block] + causal[...] if c == 0 else s[block]
            w = jnp.exp2(t * scale - lse_ref[:, here])
            weights[block, here] = w
            rounded[block, here] = w.astype(BF16)
    values_t = values[...].T
    keys_t = keys[...].T
    out_t[...] = dot(values_t, rounded[...])
    dots = []
    for h in range(PER):
        here = slice(h * rows, (h + 1) * rows)
        dots.append(jnp.sum(gt_ref[:, here].astype(F32) * out_t[:, here], axis=0, keepdims=True))
    for h in range(PER):
        here = slice(h * rows, (h + 1) * rows)
        pressure = dot(values[...], gt_ref[:, here])
        slopes[:, here] = (weights[:, here] * (pressure - dots[h]) * inverse_root).astype(BF16)
    dq_t = dot(keys_t, slopes[...])
    live = lax.broadcasted_iota(jnp.int32, (rows, HEAD_SIZE), 0) < lengths_ref[0, own]
    for h in range(PER):
        cols = slice(h * HEAD_SIZE, (h + 1) * HEAD_SIZE)
        here = slice(h * rows, (h + 1) * rows)
        done[1, :, cols] = dq_t[:, here].T.astype(BF16)
        done[0, :, cols] = jnp.where(live, out_t[:, here].T, 0.0).astype(BF16)
    wide = PER * HEAD_SIZE
    copies = [
        pltpu.make_async_copy(done.at[i], out.at[:, group * wide : (group + 1) * wide], sems.at[i])
        for i, out in enumerate(outs)
    ]
    for copy in copies:
        copy.start()
    for copy in copies:
        copy.wait()


def attend(slots, group, carried, parents, lengths, key_blocks, value_pair, qt, gt, lse):
    count = candidate_count(slots)
    rows = key_blocks[0].shape[0]
    lanes = PER * rows
    inverse_root = HEAD_SIZE ** (-0.5)
    smem = pl.BlockSpec(memory_space=pltpu.SMEM)
    vm = pl.BlockSpec(memory_space=pltpu.VMEM)
    anywhere = pl.BlockSpec(memory_space=pl.ANY)
    first = 7 + count
    return pl.pallas_call(
        functools.partial(attend_kernel, slots, group, LOG2E * inverse_root, inverse_root),
        name="attend",
        out_shape=(jax.ShapeDtypeStruct((rows, HQ * HEAD_SIZE), BF16),) * 2,
        in_specs=[smem, smem] + [vm] * (count + 5) + [anywhere] * len(carried),
        out_specs=(anywhere, anywhere),
        scratch_shapes=[
            pltpu.SMEM((count,), jnp.int32),
            pltpu.VMEM((count * rows, HEAD_SIZE), BF16),
            pltpu.VMEM((count * rows, HEAD_SIZE), BF16),
            pltpu.VMEM((count * rows, lanes), F32),
            pltpu.VMEM((count * rows, lanes), BF16),
            pltpu.VMEM((count * rows, lanes), BF16),
            pltpu.VMEM((count * rows, rows), BF16),
            pltpu.VMEM((rows, rows), F32),
            pltpu.VMEM((HEAD_SIZE, lanes), F32),
            pltpu.VMEM((2, rows, PER * HEAD_SIZE), BF16),
            pltpu.SemaphoreType.DMA((2,)),
        ],
        input_output_aliases={first + i: i for i in range(len(carried))},
        compiler_params=pltpu.CompilerParams(vmem_limit_bytes=SMALL_LIMIT),
        cost_estimate=pl.CostEstimate(flops=800_000_000, bytes_accessed=1_500_000, transcendentals=700_000),
    )(parents, lengths, *key_blocks, *value_pair, qt, gt, lse, *carried)


def gradient_kernel(slots, factor, received_ref, x_ref, part_ref, low_ref, keep_ref, send_ref):
    rows, width = x_ref.shape
    core = lax.axis_index("rep")
    half = keep_ref.shape[1]
    start = width - half
    own = lax.axis_index("node")
    total = received_ref[own]
    for slot in range(slots):
        total += jnp.where(slot > own, received_ref[slot], 0.0)
    total = total.astype(BF16)

    def place(ref, which):
        if which == 0:
            ref[...] = dot(total, x_ref[:, :half]) * factor
        else:
            ref[:, :start] = dot(total, x_ref[:, half:]) * factor

    for mine in range(2):

        @pl.when(core == mine)
        def _():
            place(send_ref, 1 - mine)
            place(keep_ref, mine)

    low_t = [low_ref[...]]
    for c in range(1, part_ref.shape[1] // rows):
        low_t.append(received_ref[jnp.maximum(candidate_slot(slots, own, c), 0)].astype(BF16))
    up = dot_nt(jnp.concatenate(low_t, axis=1), part_ref[...]) * factor

    @pl.when(core == 0)
    def _():
        send_ref[:, start:] = up

    @pl.when(core == 1)
    def _():
        keep_ref[:, start:] = up


def gradients(slots, received, x, parts, low, factor):
    _, width = x.shape
    inner = parts.shape[0]
    rank = received.shape[1]
    half = (width + inner) // 2
    vm = pl.BlockSpec(memory_space=pltpu.VMEM)
    return pl.pallas_call(
        functools.partial(gradient_kernel, slots, factor),
        name="gradients",
        out_shape=(jax.ShapeDtypeStruct((rank, half), F32),) * 2,
        in_specs=[vm] * 4,
        out_specs=(vm, vm),
        compiler_params=pltpu.CompilerParams(vmem_limit_bytes=SMALL_LIMIT),
        cost_estimate=pl.CostEstimate(flops=80_000_000, bytes_accessed=4_000_000, transcendentals=0),
    )(received, x, parts, low)


def gather_keys(slots, block):
    if not paired(slots):
        return candidate_blocks(slots, block)
    columns = {0: block}
    for d in range(slots // 2 - 1, 0, -1):
        columns[d] = lax.ppermute(block, "node", [(i, i + 2 * d) for i in range(slots - 2 * d)])
    blocks = []
    for d in range(slots // 2):
        swap = [(i, i ^ 1) for i in range(2 * d, slots) if d or i % 2 == 0]
        blocks += [columns[d], lax.ppermute(columns[d], "node", swap)]
    return blocks


def candidate_blocks(slots, block):
    own = lax.axis_index("node")
    whole = lax.all_gather(block, "node")
    return [block] + [
        lax.dynamic_index_in_dim(whole, jnp.maximum(candidate_slot(slots, own, c), 0), 0, keepdims=False)
        for c in range(1, candidate_count(slots))
    ]


def gather_values(slots, message):
    if not paired(slots):
        blocks = candidate_blocks(slots, message[0])
        return jnp.stack(blocks[0::2]), jnp.stack(blocks[1::2])
    even = lax.all_to_all(
        message, "node", 0, 0, axis_index_groups=[list(range(y, slots, 2)) for y in range(2)]
    )
    odd = lax.ppermute(even, "node", [(i, i ^ 1) for i in range(slots)])
    return even, odd


def sum_over_all(slots, keep, send):
    core = lax.axis_index("rep")
    own = lax.axis_index("node")
    swap_core = [(0, 1), (1, 0)]

    def swap(x, bit):
        return lax.ppermute(x, "node", [(i, i ^ bit) for i in range(slots)])

    came = lax.ppermute(send, "rep", swap_core)
    total = keep + came
    quarter = total.shape[1] // 2
    low, high = total[:, :quarter], total[:, quarter:]
    odd = own % 2 == 1
    mine = jnp.where(odd, high, low)
    other = jnp.where(odd, low, high).astype(BF16)
    mine = (mine + swap(other, 1).astype(F32)).astype(BF16)
    bit = 2
    while bit < slots:
        mine = (mine.astype(F32) + swap(mine, bit).astype(F32)).astype(BF16)
        bit *= 2
    other = swap(mine, 1)
    half = jnp.concatenate([jnp.where(odd, other, mine), jnp.where(odd, mine, other)], axis=1)
    other = lax.ppermute(half, "rep", swap_core)
    second = core == 1
    whole = jnp.concatenate([jnp.where(second, other, half), jnp.where(second, half, other)], axis=1)
    return whole.astype(F32)


def on_device(
    normed_input,
    queries,
    rotated_key_heads,
    frozen_value_rows,
    adapter_down_weight,
    adapter_up_weight,
    output_gradient,
    parents,
    lengths,
):
    x = normed_input[0]
    rows, width = x.shape
    slots = lax.axis_size("node")
    key_blocks = gather_keys(slots, rotated_key_heads[0])
    message, low, qt, gt = prepare(
        slots // 2 if paired(slots) else 1,
        lengths,
        x,
        adapter_down_weight.T,
        adapter_up_weight,
        frozen_value_rows[0],
        queries[0],
        output_gradient[0],
    )
    value_pair = gather_values(slots, message)
    projected, parts, lse = stats(slots, parents, lengths, key_blocks, qt, gt, adapter_up_weight, low)
    received = lax.all_to_all(projected, "node", 0, 0)
    factor = (slots * lax.axis_size("rep") * rows) ** (-0.5)
    keep, send = gradients(slots, received, x, parts, low, factor)
    whole = sum_over_all(slots, keep, send)
    carried = ()
    for group in range(KEY_HEADS):
        carried = attend(slots, group, carried, parents, lengths, key_blocks, value_pair, qt, gt, lse)
    attended, query_grad = carried
    return (attended[None], query_grad[None], whole[:, :width].T, whole[:, width:])


def solution(mesh):
    tokens = P(("groups", "rep"), "node", None)
    trees = P(("groups", "rep"), None)
    return jax.shard_map(
        on_device,
        mesh=mesh,
        in_specs=(tokens,) * 4 + (P(), P()) + (tokens, trees, trees),
        out_specs=(tokens, tokens, P("groups", None), P("groups", None)),
        check_vma=False,
    )
```

```python
import functools

import jax
import jax.numpy as jnp
from jax import lax
from jax.experimental import pallas as pl
from jax.experimental.pallas import tpu as pltpu
from jax.sharding import PartitionSpec as P


HQ = 20
KEY_HEADS = 4
HEAD_SIZE = 128
PROMPT = 2
SPAN = 5
PER = HQ // KEY_HEADS

NEGATIVE = -1e30
LOG2E = 1.4426950408889634
F32 = jnp.float32
BF16 = jnp.bfloat16


VMEM_LIMIT = 56 * 1024 * 1024
SMALL_LIMIT = 16 * 1024 * 1024


def dot(a, b):
    return lax.dot_general(a, b, (((1,), (0,)), ((), ())), preferred_element_type=F32)


def dot_nt(a, b):
    return lax.dot_general(a, b, (((1,), (1,)), ((), ())), preferred_element_type=F32)


def dot_tn(a, b):
    return lax.dot_general(a, b, (((0,), (0,)), ((), ())), preferred_element_type=F32)


def paired(slots):
    return slots % 2 == 0 and slots <= 1 + PROMPT + SPAN


def candidate_count(slots):
    return slots if paired(slots) else 1 + PROMPT + SPAN


def candidate_slot(slots, own, c):
    if paired(slots):
        pair = own - (c // 2) * 2
        slot = pair + (c % 2) * (1 - 2 * (pair % 2))
        return jnp.where(pair >= 0, slot, -1)
    window = own - c
    window = jnp.where(window >= PROMPT, window, -1)
    prompt = c - SPAN - 1
    prompt = jnp.where(prompt < own, prompt, -1)
    return jnp.where(c == 0, own, jnp.where(c <= SPAN, window, prompt))


def value_index(slots, own, j):
    return jnp.maximum(own // 2 - j, 0) if paired(slots) else j


def mark_candidates(slots, parents_ref, lengths_ref, live_ref):
    own = lax.axis_index("node")
    count = candidate_count(slots)
    for c in range(count):
        live_ref[c] = 0
    live_ref[0] = lengths_ref[0, own]

    def climb(step, current):
        at = jnp.maximum(current, 0)
        for c in range(1, count):
            slot = candidate_slot(slots, own, c)

            @pl.when((slot == current) & (current >= 0))
            def _():
                live_ref[c] = lengths_ref[0, at]

        return jnp.where(current >= 0, parents_ref[0, at], -1)

    lax.fori_loop(0, PROMPT + SPAN, climb, parents_ref[0, own])


def copies_of(pairs, sems, first=0):
    copies = [pltpu.make_async_copy(source, target, sems.at[first + i]) for i, (source, target) in enumerate(pairs)]
    for copy in copies:
        copy.start()
    return copies


def prepare_kernel(
    lengths_ref, x_ref, down_ref, up_ref, frozen_ref, q_ref, g_ref,
    message_ref, low_ref, qt_ref, gt_ref,
):
    own = lax.axis_index("node")
    rows = x_ref.shape[0]
    low_t = dot_nt(down_ref[...], x_ref[...]).astype(BF16)
    values = frozen_ref[...].astype(F32) + dot_tn(low_t, up_ref[...])
    low_ref[...] = low_t
    for i in range(message_ref.shape[0]):
        message_ref[i] = values.astype(BF16)
    length = lengths_ref[0, own]
    live = lax.broadcasted_iota(jnp.int32, (rows, HEAD_SIZE), 0) < length
    for h in range(HQ):
        cols = slice(h * HEAD_SIZE, (h + 1) * HEAD_SIZE)
        here = slice(h * rows, (h + 1) * rows)
        qt_ref[:, here] = q_ref[:, cols].T
        g = jnp.where(live, g_ref[:, cols].astype(F32), 0.0).astype(BF16)
        gt_ref[:, here] = g.T


def prepare(copies, lengths, x, down_t, up, frozen, q, g):
    rows = x.shape[0]
    rank, width = up.shape
    vm = pl.BlockSpec(memory_space=pltpu.VMEM)
    return pl.pallas_call(
        prepare_kernel,
        name="prepare",
        out_shape=(
            jax.ShapeDtypeStruct((copies, rows, width), BF16),
            jax.ShapeDtypeStruct((rank, rows), BF16),
            jax.ShapeDtypeStruct((HEAD_SIZE, HQ * rows), BF16),
            jax.ShapeDtypeStruct((HEAD_SIZE, HQ * rows), BF16),
        ),
        in_specs=[pl.BlockSpec(memory_space=pltpu.SMEM)] + [vm] * 6,
        out_specs=(vm,) * 4,
        compiler_params=pltpu.CompilerParams(vmem_limit_bytes=VMEM_LIMIT),
        cost_estimate=pl.CostEstimate(flops=100_000_000, bytes_accessed=6_000_000, transcendentals=0),
    )(lengths, x, down_t, up, frozen, q, g)


def fill_masks(live_ref, mask_ref, causal_ref):
    rows = causal_ref.shape[0]
    key_at = lax.broadcasted_iota(jnp.int32, (rows, rows), 0)
    across = lax.broadcasted_iota(jnp.int32, (rows, rows), 1)
    for c in range(live_ref.shape[0]):
        dead = (across == 0) & (key_at >= live_ref[c])
        mask_ref[c * rows : (c + 1) * rows] = jnp.where(dead, NEGATIVE, 0.0).astype(BF16)
    causal_ref[...] = jnp.where(key_at <= across, 0.0, NEGATIVE)


def first_row(rows, lanes):
    return jnp.where(lax.broadcasted_iota(jnp.int32, (rows, lanes), 0) == 0, 1.0, 0.0).astype(BF16)


def fill_bias(live_ref, bias_ref):
    rows = bias_ref.shape[1]
    key_at = lax.broadcasted_iota(jnp.int32, (rows, rows), 0)
    query_at = lax.broadcasted_iota(jnp.int32, (rows, rows), 1)
    for c in range(live_ref.shape[0]):
        allowed = key_at < live_ref[c]
        if c == 0:
            allowed &= key_at <= query_at
        bias_ref[c] = jnp.where(allowed, 0.0, NEGATIVE)


def fold(x, op):
    return op(x.reshape(x.shape[0] // 8, 8, x.shape[1]), axis=0)


def stats_kernel(slots, scale, *refs):
    count = candidate_count(slots)
    parents_ref, lengths_ref = refs[:2]
    key_refs = refs[2 : 2 + count]
    qt_ref, gt_ref, up_ref, low_ref = refs[2 + count : 6 + count]
    proj_ref, part_ref, lse_ref = refs[6 + count : 9 + count]
    live_ref, keys, weights, bias, scores, shares, rest = refs[9 + count :]
    rows = key_refs[0].shape[0]
    own = lax.axis_index("node")
    mark_candidates(slots, parents_ref, lengths_ref, live_ref)
    fill_bias(live_ref, bias)
    for c in range(count):
        keys[c * rows : (c + 1) * rows] = key_refs[c][...]

    def lanes_of(h):
        return pl.ds(pl.multiple_of(h * rows, rows), rows)

    def step(it, carried):
        top, inverse = carried
        here = jnp.minimum(it, HQ - 1)
        before = jnp.clip(it - 1, 0, HQ - 1)
        last = jnp.maximum(it - 2, 0)
        columns = pl.ds(pl.multiple_of((here // PER) * HEAD_SIZE, HEAD_SIZE), HEAD_SIZE)
        q = qt_ref[:, lanes_of(here)]
        high = summed = None
        fresh = dot(keys[:, columns], q)
        for c in range(count):
            block = slice(c * rows, (c + 1) * rows)
            weights[block, lanes_of(last)] = (shares[block] * inverse).astype(BF16)
            p = jnp.exp2(scores[block] * scale - top)
            shares[block] = p
            part = fold(p, jnp.sum)
            summed = part if c == 0 else summed + part
            s = fresh[block] + bias[c]
            scores[block] = s
            most = fold(s, jnp.max)
            high = most if c == 0 else jnp.maximum(high, most)
        total = jnp.sum(summed, axis=0, keepdims=True)
        lse_ref[:, lanes_of(before)] = top + jnp.log2(total)
        return jnp.max(high, axis=0, keepdims=True) * scale, 1.0 / total

    empty = jnp.zeros((1, rows), F32)
    lax.fori_loop(0, HQ + 2, step, (empty, empty), unroll=2)
    for k in range(KEY_HEADS):
        lanes = slice(k * PER * rows, (k + 1) * PER * rows)
        cols = slice(k * HEAD_SIZE, (k + 1) * HEAD_SIZE)
        part = dot_nt(gt_ref[:, lanes], weights[:, lanes])
        high = part.astype(BF16)
        part_ref[cols] = high
        rest[cols] = (part - high.astype(F32)).astype(BF16)
    up = up_ref[...]
    proj = dot(up, part_ref[...]) + dot(up, rest[...])
    low = low_ref[...].astype(F32)
    for slot in range(slots):
        proj_ref[slot] = jnp.where(slot > own, low, 0.0)
    for c in range(count):

        @pl.when(live_ref[c] > 0)
        def _():
            proj_ref[candidate_slot(slots, own, c)] = proj[:, c * rows : (c + 1) * rows]


def stats(slots, parents, lengths, key_blocks, qt, gt, up, low):
    count = candidate_count(slots)
    rows, width = key_blocks[0].shape
    rank = up.shape[0]
    scale = LOG2E * HEAD_SIZE ** (-0.5)
    smem = pl.BlockSpec(memory_space=pltpu.SMEM)
    vm = pl.BlockSpec(memory_space=pltpu.VMEM)
    return pl.pallas_call(
        functools.partial(stats_kernel, slots, scale),
        name="stats",
        out_shape=(
            jax.ShapeDtypeStruct((slots, rank, rows), F32),
            jax.ShapeDtypeStruct((width, count * rows), BF16),
            jax.ShapeDtypeStruct((1, HQ * rows), F32),
        ),
        in_specs=[smem, smem] + [vm] * (count + 4),
        out_specs=(vm, vm, vm),
        scratch_shapes=[
            pltpu.SMEM((count,), jnp.int32),
            pltpu.VMEM((count * rows, width), BF16),
            pltpu.VMEM((count * rows, HQ * rows), BF16),
            pltpu.VMEM((count, rows, rows), F32),
            pltpu.VMEM((count * rows, rows), F32),
            pltpu.VMEM((count * rows, rows), F32),
            pltpu.VMEM((width, count * rows), BF16),
        ],
        compiler_params=pltpu.CompilerParams(vmem_limit_bytes=VMEM_LIMIT),
        cost_estimate=pl.CostEstimate(flops=2_000_000_000, bytes_accessed=5_000_000, transcendentals=3_000_000),
    )(parents, lengths, *key_blocks, qt, gt, up, low)


def attend_kernel(slots, group, scale, inverse_root, *refs):
    count = candidate_count(slots)
    parents_ref, lengths_ref = refs[:2]
    key_refs = refs[2 : 2 + count]
    value_refs = refs[2 + count : 4 + count]
    qt_ref, gt_ref, lse_ref = refs[4 + count : 7 + count]
    outs = refs[-13:-11]
    live_ref, keys, values, weights, rounded, slopes, masks, causal, out_t, done, sems = refs[-11:]
    rows = key_refs[0].shape[0]
    head = slice(group * HEAD_SIZE, (group + 1) * HEAD_SIZE)
    qt_ref, gt_ref, lse_ref = (
        ref.at[:, group * PER * rows : (group + 1) * PER * rows] for ref in (qt_ref, gt_ref, lse_ref)
    )
    own = lax.axis_index("node")
    mark_candidates(slots, parents_ref, lengths_ref, live_ref)
    fill_masks(live_ref, masks, causal)
    ones = first_row(HEAD_SIZE, rows)
    for c in range(count):
        block = slice(c * rows, (c + 1) * rows)
        keys[block] = key_refs[c][:, head]
        values[block] = value_refs[c % 2][value_index(slots, own, c // 2), :, head]
    for h in range(PER):
        here = slice(h * rows, (h + 1) * rows)
        s = dot(
            jnp.concatenate([keys[...], masks[...]], axis=1), jnp.concatenate([qt_ref[:, here], ones], axis=0)
        )
        for c in range(count):
            block = slice(c * rows, (c + 1) * rows)
            t = s[block] + causal[...] if c == 0 else s[block]
            w = jnp.exp2(t * scale - lse_ref[:, here])
            weights[block, here] = w
            rounded[block, here] = w.astype(BF16)
    values_t = values[...].T
    keys_t = keys[...].T
    out_t[...] = dot(values_t, rounded[...])
    dots = []
    for h in range(PER):
        here = slice(h * rows, (h + 1) * rows)
        dots.append(jnp.sum(gt_ref[:, here].astype(F32) * out_t[:, here], axis=0, keepdims=True))
    for h in range(PER):
        here = slice(h * rows, (h + 1) * rows)
        pressure = dot(values[...], gt_ref[:, here])
        slopes[:, here] = (weights[:, here] * (pressure - dots[h]) * inverse_root).astype(BF16)
    dq_t = dot(keys_t, slopes[...])
    live = lax.broadcasted_iota(jnp.int32, (rows, HEAD_SIZE), 0) < lengths_ref[0, own]
    for h in range(PER):
        cols = slice(h * HEAD_SIZE, (h + 1) * HEAD_SIZE)
        here = slice(h * rows, (h + 1) * rows)
        done[1, :, cols] = dq_t[:, here].T.astype(BF16)
        done[0, :, cols] = jnp.where(live, out_t[:, here].T, 0.0).astype(BF16)
    wide = PER * HEAD_SIZE
    copies = [
        pltpu.make_async_copy(done.at[i], out.at[:, group * wide : (group + 1) * wide], sems.at[i])
        for i, out in enumerate(outs)
    ]
    for copy in copies:
        copy.start()
    for copy in copies:
        copy.wait()


def attend(slots, group, carried, parents, lengths, key_blocks, value_pair, qt, gt, lse):
    count = candidate_count(slots)
    rows = key_blocks[0].shape[0]
    lanes = PER * rows
    inverse_root = HEAD_SIZE ** (-0.5)
    smem = pl.BlockSpec(memory_space=pltpu.SMEM)
    vm = pl.BlockSpec(memory_space=pltpu.VMEM)
    anywhere = pl.BlockSpec(memory_space=pl.ANY)
    first = 7 + count
    return pl.pallas_call(
        functools.partial(attend_kernel, slots, group, LOG2E * inverse_root, inverse_root),
        name="attend",
        out_shape=(jax.ShapeDtypeStruct((rows, HQ * HEAD_SIZE), BF16),) * 2,
        in_specs=[smem, smem] + [vm] * (count + 5) + [anywhere] * len(carried),
        out_specs=(anywhere, anywhere),
        scratch_shapes=[
            pltpu.SMEM((count,), jnp.int32),
            pltpu.VMEM((count * rows, HEAD_SIZE), BF16),
            pltpu.VMEM((count * rows, HEAD_SIZE), BF16),
            pltpu.VMEM((count * rows, lanes), F32),
            pltpu.VMEM((count * rows, lanes), BF16),
            pltpu.VMEM((count * rows, lanes), BF16),
            pltpu.VMEM((count * rows, rows), BF16),
            pltpu.VMEM((rows, rows), F32),
            pltpu.VMEM((HEAD_SIZE, lanes), F32),
            pltpu.VMEM((2, rows, PER * HEAD_SIZE), BF16),
            pltpu.SemaphoreType.DMA((2,)),
        ],
        input_output_aliases={first + i: i for i in range(len(carried))},
        compiler_params=pltpu.CompilerParams(vmem_limit_bytes=SMALL_LIMIT),
        cost_estimate=pl.CostEstimate(flops=800_000_000, bytes_accessed=1_500_000, transcendentals=700_000),
    )(parents, lengths, *key_blocks, *value_pair, qt, gt, lse, *carried)


def gradient_kernel(slots, factor, received_hbm, x_ref, part_ref, low_ref, keep_hbm, send_hbm, received_ref, halves, sems):
    width = x_ref.shape[1]
    core = lax.axis_index("rep")
    own = lax.axis_index("node")
    half = halves.shape[2]
    start = width - half
    (arrival,) = copies_of([(received_hbm, received_ref)], sems)
    arrival.wait()
    total = received_ref[own]
    for slot in range(slots):
        total += jnp.where(slot > own, received_ref[slot], 0.0)
    total = total.astype(BF16)
    low_t = [low_ref[...]]
    for c in range(1, part_ref.shape[1] // low_ref.shape[1]):
        low_t.append(received_ref[jnp.maximum(candidate_slot(slots, own, c), 0)].astype(BF16))
    low_t = jnp.concatenate(low_t, axis=1)

    def place(which):
        if which == 0:
            halves[0] = dot(total, x_ref[:, :half]) * factor
        else:
            halves[1, :, :start] = dot(total, x_ref[:, half:]) * factor
            halves[1, :, start:] = dot_nt(low_t, part_ref[...]) * factor

    for mine in range(2):

        @pl.when(core == mine)
        def _():
            place(1 - mine)
            (sent,) = copies_of([(halves.at[1 - mine], send_hbm)], sems, 1)
            place(mine)
            (kept,) = copies_of([(halves.at[mine], keep_hbm)], sems, 2)
            sent.wait()
            kept.wait()


def gradients(slots, received, x, parts, low, factor):
    _, width = x.shape
    inner = parts.shape[0]
    rank = received.shape[1]
    half = (width + inner) // 2
    vm = pl.BlockSpec(memory_space=pltpu.VMEM)
    anywhere = pl.BlockSpec(memory_space=pltpu.HBM)
    return pl.pallas_call(
        functools.partial(gradient_kernel, slots, factor),
        name="gradients",
        out_shape=(jax.ShapeDtypeStruct((rank, half), F32),) * 2,
        in_specs=[anywhere] + [vm] * 3,
        out_specs=(anywhere, anywhere),
        scratch_shapes=[
            pltpu.VMEM(received.shape, F32),
            pltpu.VMEM((2, rank, half), F32),
            pltpu.SemaphoreType.DMA((3,)),
        ],
        compiler_params=pltpu.CompilerParams(vmem_limit_bytes=SMALL_LIMIT),
        cost_estimate=pl.CostEstimate(flops=80_000_000, bytes_accessed=4_000_000, transcendentals=0),
    )(received, x, parts, low)


def finish_kernel(half_ref, other_ref, down_hbm, up_hbm, whole, sems):
    core = lax.axis_index("rep")
    half = half_ref.shape[1]
    width = down_hbm.shape[1]

    @pl.when(core == 0)
    def _():
        whole[:, :half] = half_ref[...].astype(F32)
        whole[:, half:] = other_ref[...].astype(F32)

    @pl.when(core == 1)
    def _():
        whole[:, :half] = other_ref[...].astype(F32)
        whole[:, half:] = half_ref[...].astype(F32)

    for copy in copies_of([(whole.at[:, :width], down_hbm), (whole.at[:, width:], up_hbm)], sems):
        copy.wait()


def finish(half, other, width):
    rank, columns = half.shape
    vm = pl.BlockSpec(memory_space=pltpu.VMEM)
    anywhere = pl.BlockSpec(memory_space=pltpu.HBM)
    return pl.pallas_call(
        finish_kernel,
        name="finish",
        out_shape=(
            jax.ShapeDtypeStruct((rank, width), F32),
            jax.ShapeDtypeStruct((rank, 2 * columns - width), F32),
        ),
        in_specs=[vm, vm],
        out_specs=(anywhere, anywhere),
        scratch_shapes=[pltpu.VMEM((rank, 2 * columns), F32), pltpu.SemaphoreType.DMA((2,))],
        compiler_params=pltpu.CompilerParams(vmem_limit_bytes=SMALL_LIMIT),
    )(half, other)


def gather_keys(slots, block):
    if not paired(slots):
        return candidate_blocks(slots, block)
    columns = {0: block}
    for d in range(slots // 2 - 1, 0, -1):
        columns[d] = lax.ppermute(block, "node", [(i, i + 2 * d) for i in range(slots - 2 * d)])
    blocks = []
    for d in range(slots // 2):
        swap = [(i, i ^ 1) for i in range(slots)]
        blocks += [columns[d], lax.ppermute(columns[d], "node", swap)]
    return blocks


def candidate_blocks(slots, block):
    own = lax.axis_index("node")
    whole = lax.all_gather(block, "node")
    return [block] + [
        lax.dynamic_index_in_dim(whole, jnp.maximum(candidate_slot(slots, own, c), 0), 0, keepdims=False)
        for c in range(1, candidate_count(slots))
    ]


def gather_values(slots, message):
    if not paired(slots):
        blocks = candidate_blocks(slots, message[0])
        return jnp.stack(blocks[0::2]), jnp.stack(blocks[1::2])
    even = lax.all_to_all(
        message, "node", 0, 0, axis_index_groups=[list(range(y, slots, 2)) for y in range(2)]
    )
    odd = lax.ppermute(even, "node", [(i, i ^ 1) for i in range(slots)])
    return even, odd


def sum_over_all(slots, keep, send, width):
    own = lax.axis_index("node")
    swap_core = [(0, 1), (1, 0)]

    def swap(x, bit):
        return lax.ppermute(x, "node", [(i, i ^ bit) for i in range(slots)])

    came = lax.ppermute(send, "rep", swap_core)
    total = keep + came
    quarter = total.shape[1] // 2
    low, high = total[:, :quarter], total[:, quarter:]
    odd = own % 2 == 1
    mine = jnp.where(odd, high, low)
    other = jnp.where(odd, low, high).astype(BF16)
    mine = (mine + swap(other, 1).astype(F32)).astype(BF16)
    bit = 2
    while bit < slots:
        mine = (mine.astype(F32) + swap(mine, bit).astype(F32)).astype(BF16)
        bit *= 2
    other = swap(mine, 1)
    half = jnp.concatenate([jnp.where(odd, other, mine), jnp.where(odd, mine, other)], axis=1)
    other = lax.ppermute(half, "rep", swap_core)
    return finish(half, other, width)


def on_device(
    normed_input,
    queries,
    rotated_key_heads,
    frozen_value_rows,
    adapter_down_weight,
    adapter_up_weight,
    output_gradient,
    parents,
    lengths,
):
    x = normed_input[0]
    rows, width = x.shape
    slots = lax.axis_size("node")
    key_blocks = gather_keys(slots, rotated_key_heads[0])
    message, low, qt, gt = prepare(
        slots // 2 if paired(slots) else 1,
        lengths,
        x,
        adapter_down_weight.T,
        adapter_up_weight,
        frozen_value_rows[0],
        queries[0],
        output_gradient[0],
    )
    value_pair = gather_values(slots, message)
    projected, parts, lse = stats(slots, parents, lengths, key_blocks, qt, gt, adapter_up_weight, low)
    received = lax.all_to_all(projected, "node", 0, 0)
    factor = (slots * lax.axis_size("rep") * rows) ** (-0.5)
    keep, send = gradients(slots, received, x, parts, low, factor)
    down_grad, up_grad = sum_over_all(slots, keep, send, width)
    carried = ()
    for group in range(KEY_HEADS):
        carried = attend(slots, group, carried, parents, lengths, key_blocks, value_pair, qt, gt, lse)
    attended, query_grad = carried
    return (attended[None], query_grad[None], down_grad.T, up_grad)


def solution(mesh):
    tokens = P(("groups", "rep"), "node", None)
    trees = P(("groups", "rep"), None)
    return jax.shard_map(
        on_device,
        mesh=mesh,
        in_specs=(tokens,) * 4 + (P(), P()) + (tokens, trees, trees),
        out_specs=(tokens, tokens, P("groups", None), P("groups", None)),
        check_vma=False,
    )
```

```python
import functools

import jax
import jax.numpy as jnp
from jax import lax
from jax.experimental import pallas as pl
from jax.experimental.pallas import tpu as pltpu
from jax.sharding import PartitionSpec as P


HQ = 20
KEY_HEADS = 4
HEAD_SIZE = 128
PROMPT = 2
SPAN = 5
PER = HQ // KEY_HEADS

NEGATIVE = -1e30
LOG2E = 1.4426950408889634
F32 = jnp.float32
BF16 = jnp.bfloat16


VMEM_LIMIT = 56 * 1024 * 1024
SMALL_LIMIT = 16 * 1024 * 1024


def dot(a, b):
    return lax.dot_general(a, b, (((1,), (0,)), ((), ())), preferred_element_type=F32)


def dot_nt(a, b):
    return lax.dot_general(a, b, (((1,), (1,)), ((), ())), preferred_element_type=F32)


def dot_tn(a, b):
    return lax.dot_general(a, b, (((0,), (0,)), ((), ())), preferred_element_type=F32)


def paired(slots):
    return slots % 2 == 0 and slots <= 1 + PROMPT + SPAN


def candidate_count(slots):
    return slots if paired(slots) else 1 + PROMPT + SPAN


def candidate_slot(slots, own, c):
    if paired(slots):
        pair = own - (c // 2) * 2
        slot = pair + (c % 2) * (1 - 2 * (pair % 2))
        return jnp.where(pair >= 0, slot, -1)
    window = own - c
    window = jnp.where(window >= PROMPT, window, -1)
    prompt = c - SPAN - 1
    prompt = jnp.where(prompt < own, prompt, -1)
    return jnp.where(c == 0, own, jnp.where(c <= SPAN, window, prompt))


def value_index(slots, own, j):
    return jnp.maximum(own // 2 - j, 0) if paired(slots) else j


def mark_candidates(slots, parents_ref, lengths_ref, live_ref):
    own = lax.axis_index("node")
    count = candidate_count(slots)
    for c in range(count):
        live_ref[c] = 0
    live_ref[0] = lengths_ref[0, own]

    def climb(step, current):
        at = jnp.maximum(current, 0)
        for c in range(1, count):
            slot = candidate_slot(slots, own, c)

            @pl.when((slot == current) & (current >= 0))
            def _():
                live_ref[c] = lengths_ref[0, at]

        return jnp.where(current >= 0, parents_ref[0, at], -1)

    lax.fori_loop(0, PROMPT + SPAN, climb, parents_ref[0, own])


def copies_of(pairs, sems, first=0):
    copies = [pltpu.make_async_copy(source, target, sems.at[first + i]) for i, (source, target) in enumerate(pairs)]
    for copy in copies:
        copy.start()
    return copies


def prepare_kernel(
    lengths_ref, x_ref, down_ref, up_ref, frozen_ref, q_ref, g_ref,
    message_ref, low_ref, qt_ref, gt_ref,
):
    own = lax.axis_index("node")
    rows = x_ref.shape[0]
    low_t = dot_nt(down_ref[...], x_ref[...]).astype(BF16)
    values = frozen_ref[...].astype(F32) + dot_tn(low_t, up_ref[...])
    low_ref[...] = low_t
    for i in range(message_ref.shape[0]):
        message_ref[i] = values.astype(BF16)
    length = lengths_ref[0, own]
    live = lax.broadcasted_iota(jnp.int32, (rows, HEAD_SIZE), 0) < length
    for h in range(HQ):
        cols = slice(h * HEAD_SIZE, (h + 1) * HEAD_SIZE)
        here = slice(h * rows, (h + 1) * rows)
        qt_ref[:, here] = q_ref[:, cols].T
        g = jnp.where(live, g_ref[:, cols].astype(F32), 0.0).astype(BF16)
        gt_ref[:, here] = g.T


def prepare(copies, lengths, x, down_t, up, frozen, q, g):
    rows = x.shape[0]
    rank, width = up.shape
    vm = pl.BlockSpec(memory_space=pltpu.VMEM)
    return pl.pallas_call(
        prepare_kernel,
        name="prepare",
        out_shape=(
            jax.ShapeDtypeStruct((copies, rows, width), BF16),
            jax.ShapeDtypeStruct((rank, rows), BF16),
            jax.ShapeDtypeStruct((HEAD_SIZE, HQ * rows), BF16),
            jax.ShapeDtypeStruct((HEAD_SIZE, HQ * rows), BF16),
        ),
        in_specs=[pl.BlockSpec(memory_space=pltpu.SMEM)] + [vm] * 6,
        out_specs=(vm,) * 4,
        compiler_params=pltpu.CompilerParams(vmem_limit_bytes=VMEM_LIMIT),
        cost_estimate=pl.CostEstimate(flops=100_000_000, bytes_accessed=6_000_000, transcendentals=0),
    )(lengths, x, down_t, up, frozen, q, g)


def fill_masks(live_ref, mask_ref, causal_ref):
    rows = causal_ref.shape[0]
    key_at = lax.broadcasted_iota(jnp.int32, (rows, rows), 0)
    across = lax.broadcasted_iota(jnp.int32, (rows, rows), 1)
    for c in range(live_ref.shape[0]):
        dead = (across == 0) & (key_at >= live_ref[c])
        mask_ref[c * rows : (c + 1) * rows] = jnp.where(dead, NEGATIVE, 0.0).astype(BF16)
    causal_ref[...] = jnp.where(key_at <= across, 0.0, NEGATIVE)


def first_row(rows, lanes):
    return jnp.where(lax.broadcasted_iota(jnp.int32, (rows, lanes), 0) == 0, 1.0, 0.0).astype(BF16)


def fill_bias(live_ref, bias_ref):
    rows = bias_ref.shape[1]
    key_at = lax.broadcasted_iota(jnp.int32, (rows, rows), 0)
    query_at = lax.broadcasted_iota(jnp.int32, (rows, rows), 1)
    for c in range(live_ref.shape[0]):
        allowed = key_at < live_ref[c]
        if c == 0:
            allowed &= key_at <= query_at
        bias_ref[c] = jnp.where(allowed, 0.0, NEGATIVE)


def fold(x, op):
    return op(x.reshape(x.shape[0] // 8, 8, x.shape[1]), axis=0)


def stats_kernel(slots, scale, *refs):
    count = candidate_count(slots)
    parents_ref, lengths_ref = refs[:2]
    key_refs = refs[2 : 2 + count]
    qt_ref, gt_ref, up_ref, low_ref = refs[2 + count : 6 + count]
    proj_ref, part_ref, lse_ref = refs[6 + count : 9 + count]
    live_ref, keys, weights, bias, scores, shares, rest = refs[9 + count :]
    rows = key_refs[0].shape[0]
    own = lax.axis_index("node")
    mark_candidates(slots, parents_ref, lengths_ref, live_ref)
    fill_bias(live_ref, bias)
    for c in range(count):
        keys[c * rows : (c + 1) * rows] = key_refs[c][...]

    def lanes_of(h):
        return pl.ds(pl.multiple_of(h * rows, rows), rows)

    def step(it, carried):
        top, inverse = carried
        here = jnp.minimum(it, HQ - 1)
        before = jnp.clip(it - 1, 0, HQ - 1)
        last = jnp.maximum(it - 2, 0)
        columns = pl.ds(pl.multiple_of((here // PER) * HEAD_SIZE, HEAD_SIZE), HEAD_SIZE)
        q = qt_ref[:, lanes_of(here)]
        high = summed = None
        fresh = dot(keys[:, columns], q)
        for c in range(count):
            block = slice(c * rows, (c + 1) * rows)
            weights[block, lanes_of(last)] = (shares[block] * inverse).astype(BF16)
            p = jnp.exp2(scores[block] * scale - top)
            shares[block] = p
            part = fold(p, jnp.sum)
            summed = part if c == 0 else summed + part
            s = fresh[block] + bias[c]
            scores[block] = s
            most = fold(s, jnp.max)
            high = most if c == 0 else jnp.maximum(high, most)
        total = jnp.sum(summed, axis=0, keepdims=True)
        lse_ref[:, lanes_of(before)] = top + jnp.log2(total)
        return jnp.max(high, axis=0, keepdims=True) * scale, 1.0 / total

    empty = jnp.zeros((1, rows), F32)
    lax.fori_loop(0, HQ + 2, step, (empty, empty), unroll=2)
    for k in range(KEY_HEADS):
        lanes = slice(k * PER * rows, (k + 1) * PER * rows)
        cols = slice(k * HEAD_SIZE, (k + 1) * HEAD_SIZE)
        part = dot_nt(gt_ref[:, lanes], weights[:, lanes])
        high = part.astype(BF16)
        part_ref[cols] = high
        rest[cols] = (part - high.astype(F32)).astype(BF16)
    up = up_ref[...]
    proj = dot(up, part_ref[...]) + dot(up, rest[...])
    low = low_ref[...].astype(F32)
    for slot in range(slots):
        proj_ref[slot] = jnp.where(slot > own, low, 0.0)
    for c in range(count):

        @pl.when(live_ref[c] > 0)
        def _():
            proj_ref[candidate_slot(slots, own, c)] = proj[:, c * rows : (c + 1) * rows]


def stats(slots, parents, lengths, key_blocks, qt, gt, up, low):
    count = candidate_count(slots)
    rows, width = key_blocks[0].shape
    rank = up.shape[0]
    scale = LOG2E * HEAD_SIZE ** (-0.5)
    smem = pl.BlockSpec(memory_space=pltpu.SMEM)
    vm = pl.BlockSpec(memory_space=pltpu.VMEM)
    return pl.pallas_call(
        functools.partial(stats_kernel, slots, scale),
        name="stats",
        out_shape=(
            jax.ShapeDtypeStruct((slots, rank, rows), F32),
            jax.ShapeDtypeStruct((width, count * rows), BF16),
            jax.ShapeDtypeStruct((1, HQ * rows), F32),
        ),
        in_specs=[smem, smem] + [vm] * (count + 4),
        out_specs=(vm, vm, vm),
        scratch_shapes=[
            pltpu.SMEM((count,), jnp.int32),
            pltpu.VMEM((count * rows, width), BF16),
            pltpu.VMEM((count * rows, HQ * rows), BF16),
            pltpu.VMEM((count, rows, rows), F32),
            pltpu.VMEM((count * rows, rows), F32),
            pltpu.VMEM((count * rows, rows), F32),
            pltpu.VMEM((width, count * rows), BF16),
        ],
        compiler_params=pltpu.CompilerParams(vmem_limit_bytes=VMEM_LIMIT),
        cost_estimate=pl.CostEstimate(flops=2_000_000_000, bytes_accessed=5_000_000, transcendentals=3_000_000),
    )(parents, lengths, *key_blocks, qt, gt, up, low)


def attend_kernel(slots, group, scale, inverse_root, *refs):
    count = candidate_count(slots)
    parents_ref, lengths_ref = refs[:2]
    key_refs = refs[2 : 2 + count]
    value_refs = refs[2 + count : 4 + count]
    qt_ref, gt_ref, lse_ref = refs[4 + count : 7 + count]
    outs = refs[-13:-11]
    live_ref, keys, values, weights, rounded, slopes, masks, causal, out_t, done, sems = refs[-11:]
    rows = key_refs[0].shape[0]
    head = slice(group * HEAD_SIZE, (group + 1) * HEAD_SIZE)
    qt_ref, gt_ref, lse_ref = (
        ref.at[:, group * PER * rows : (group + 1) * PER * rows] for ref in (qt_ref, gt_ref, lse_ref)
    )
    own = lax.axis_index("node")
    mark_candidates(slots, parents_ref, lengths_ref, live_ref)
    fill_masks(live_ref, masks, causal)
    ones = first_row(HEAD_SIZE, rows)
    for c in range(count):
        block = slice(c * rows, (c + 1) * rows)
        keys[block] = key_refs[c][:, head]
        values[block] = value_refs[c % 2][value_index(slots, own, c // 2), :, head]
    for h in range(PER):
        here = slice(h * rows, (h + 1) * rows)
        s = dot(
            jnp.concatenate([keys[...], masks[...]], axis=1), jnp.concatenate([qt_ref[:, here], ones], axis=0)
        )
        for c in range(count):
            block = slice(c * rows, (c + 1) * rows)
            t = s[block] + causal[...] if c == 0 else s[block]
            w = jnp.exp2(t * scale - lse_ref[:, here])
            weights[block, here] = w
            rounded[block, here] = w.astype(BF16)
    values_t = values[...].T
    keys_t = keys[...].T
    out_t[...] = dot(values_t, rounded[...])
    dots = []
    for h in range(PER):
        here = slice(h * rows, (h + 1) * rows)
        dots.append(jnp.sum(gt_ref[:, here].astype(F32) * out_t[:, here], axis=0, keepdims=True))
    for h in range(PER):
        here = slice(h * rows, (h + 1) * rows)
        pressure = dot(values[...], gt_ref[:, here])
        slopes[:, here] = (weights[:, here] * (pressure - dots[h]) * inverse_root).astype(BF16)
    dq_t = dot(keys_t, slopes[...])
    live = lax.broadcasted_iota(jnp.int32, (rows, HEAD_SIZE), 0) < lengths_ref[0, own]
    for h in range(PER):
        cols = slice(h * HEAD_SIZE, (h + 1) * HEAD_SIZE)
        here = slice(h * rows, (h + 1) * rows)
        done[1, :, cols] = dq_t[:, here].T.astype(BF16)
        done[0, :, cols] = jnp.where(live, out_t[:, here].T, 0.0).astype(BF16)
    wide = PER * HEAD_SIZE
    copies = [
        pltpu.make_async_copy(done.at[i], out.at[:, group * wide : (group + 1) * wide], sems.at[i])
        for i, out in enumerate(outs)
    ]
    for copy in copies:
        copy.start()
    for copy in copies:
        copy.wait()


def attend(slots, group, carried, parents, lengths, key_blocks, value_pair, qt, gt, lse):
    count = candidate_count(slots)
    rows = key_blocks[0].shape[0]
    lanes = PER * rows
    inverse_root = HEAD_SIZE ** (-0.5)
    smem = pl.BlockSpec(memory_space=pltpu.SMEM)
    vm = pl.BlockSpec(memory_space=pltpu.VMEM)
    anywhere = pl.BlockSpec(memory_space=pl.ANY)
    first = 7 + count
    return pl.pallas_call(
        functools.partial(attend_kernel, slots, group, LOG2E * inverse_root, inverse_root),
        name="attend",
        out_shape=(jax.ShapeDtypeStruct((rows, HQ * HEAD_SIZE), BF16),) * 2,
        in_specs=[smem, smem] + [vm] * (count + 5) + [anywhere] * len(carried),
        out_specs=(anywhere, anywhere),
        scratch_shapes=[
            pltpu.SMEM((count,), jnp.int32),
            pltpu.VMEM((count * rows, HEAD_SIZE), BF16),
            pltpu.VMEM((count * rows, HEAD_SIZE), BF16),
            pltpu.VMEM((count * rows, lanes), F32),
            pltpu.VMEM((count * rows, lanes), BF16),
            pltpu.VMEM((count * rows, lanes), BF16),
            pltpu.VMEM((count * rows, rows), BF16),
            pltpu.VMEM((rows, rows), F32),
            pltpu.VMEM((HEAD_SIZE, lanes), F32),
            pltpu.VMEM((2, rows, PER * HEAD_SIZE), BF16),
            pltpu.SemaphoreType.DMA((2,)),
        ],
        input_output_aliases={first + i: i for i in range(len(carried))},
        compiler_params=pltpu.CompilerParams(vmem_limit_bytes=SMALL_LIMIT),
        cost_estimate=pl.CostEstimate(flops=800_000_000, bytes_accessed=1_500_000, transcendentals=700_000),
    )(parents, lengths, *key_blocks, *value_pair, qt, gt, lse, *carried)


def gradient_kernel(
    slots, factor, received_hbm, x_ref, part_hbm, low_ref, keep_ref, send_hbm, received_ref, part_ref, send_ref, sems
):
    width = x_ref.shape[1]
    core = lax.axis_index("rep")
    own = lax.axis_index("node")
    half = keep_ref.shape[1]
    start = width - half
    arrival, parts = copies_of([(received_hbm, received_ref), (part_hbm, part_ref)], sems)
    arrival.wait()
    total = received_ref[own]
    for slot in range(slots):
        total += jnp.where(slot > own, received_ref[slot], 0.0)
    total = total.astype(BF16)
    low_t = [low_ref[...]]
    for c in range(1, part_ref.shape[1] // low_ref.shape[1]):
        low_t.append(received_ref[jnp.maximum(candidate_slot(slots, own, c), 0)].astype(BF16))
    low_t = jnp.concatenate(low_t, axis=1)

    def place(ref):
        ref[...] = dot(total, x_ref[:, :half]) * factor

    @pl.when(core == 1)
    def _():
        place(send_ref)
        (sent,) = copies_of([(send_ref, send_hbm)], sems, 2)
        parts.wait()
        keep_ref[:, start:] = dot_nt(low_t, part_ref[...]) * factor
        keep_ref[:, :start] = dot(total, x_ref[:, half:]) * factor
        sent.wait()

    @pl.when(core == 0)
    def _():
        send_ref[:, :start] = dot(total, x_ref[:, half:]) * factor
        parts.wait()
        send_ref[:, start:] = dot_nt(low_t, part_ref[...]) * factor
        (sent,) = copies_of([(send_ref, send_hbm)], sems, 2)
        place(keep_ref)
        sent.wait()


def gradients(slots, received, x, parts, low, factor):
    _, width = x.shape
    inner = parts.shape[0]
    rank = received.shape[1]
    half = (width + inner) // 2
    vm = pl.BlockSpec(memory_space=pltpu.VMEM)
    anywhere = pl.BlockSpec(memory_space=pltpu.HBM)
    return pl.pallas_call(
        functools.partial(gradient_kernel, slots, factor),
        name="gradients",
        out_shape=(jax.ShapeDtypeStruct((rank, half), F32),) * 2,
        in_specs=[anywhere, vm, anywhere, vm],
        out_specs=(vm, anywhere),
        scratch_shapes=[
            pltpu.VMEM(received.shape, F32),
            pltpu.VMEM(parts.shape, BF16),
            pltpu.VMEM((rank, half), F32),
            pltpu.SemaphoreType.DMA((3,)),
        ],
        compiler_params=pltpu.CompilerParams(vmem_limit_bytes=SMALL_LIMIT),
        cost_estimate=pl.CostEstimate(flops=80_000_000, bytes_accessed=4_000_000, transcendentals=0),
    )(received, x, parts, low)


def finish_kernel(half_ref, other_ref, down_hbm, up_hbm, whole, sems):
    core = lax.axis_index("rep")
    half = half_ref.shape[1]
    width = down_hbm.shape[1]

    @pl.when(core == 0)
    def _():
        whole[:, :half] = half_ref[...].astype(F32)
        whole[:, half:] = other_ref[...].astype(F32)

    @pl.when(core == 1)
    def _():
        whole[:, :half] = other_ref[...].astype(F32)
        whole[:, half:] = half_ref[...].astype(F32)

    for copy in copies_of([(whole.at[:, :width], down_hbm), (whole.at[:, width:], up_hbm)], sems):
        copy.wait()


def finish(half, other, width):
    rank, columns = half.shape
    vm = pl.BlockSpec(memory_space=pltpu.VMEM)
    anywhere = pl.BlockSpec(memory_space=pltpu.HBM)
    return pl.pallas_call(
        finish_kernel,
        name="finish",
        out_shape=(
            jax.ShapeDtypeStruct((rank, width), F32),
            jax.ShapeDtypeStruct((rank, 2 * columns - width), F32),
        ),
        in_specs=[vm, vm],
        out_specs=(anywhere, anywhere),
        scratch_shapes=[pltpu.VMEM((rank, 2 * columns), F32), pltpu.SemaphoreType.DMA((2,))],
        compiler_params=pltpu.CompilerParams(vmem_limit_bytes=SMALL_LIMIT),
    )(half, other)


def gather_keys(slots, block):
    if not paired(slots):
        return candidate_blocks(slots, block)
    columns = {0: block}
    for d in range(slots // 2 - 1, 0, -1):
        columns[d] = lax.ppermute(block, "node", [(i, i + 2 * d) for i in range(slots - 2 * d)])
    blocks = []
    for d in range(slots // 2):
        swap = [(i, i ^ 1) for i in range(slots)]
        blocks += [columns[d], lax.ppermute(columns[d], "node", swap)]
    return blocks


def candidate_blocks(slots, block):
    own = lax.axis_index("node")
    whole = lax.all_gather(block, "node")
    return [block] + [
        lax.dynamic_index_in_dim(whole, jnp.maximum(candidate_slot(slots, own, c), 0), 0, keepdims=False)
        for c in range(1, candidate_count(slots))
    ]


def gather_values(slots, message):
    if not paired(slots):
        blocks = candidate_blocks(slots, message[0])
        return jnp.stack(blocks[0::2]), jnp.stack(blocks[1::2])
    even = lax.all_to_all(
        message, "node", 0, 0, axis_index_groups=[list(range(y, slots, 2)) for y in range(2)]
    )
    odd = lax.ppermute(even, "node", [(i, i ^ 1) for i in range(slots)])
    return even, odd


def sum_over_all(slots, keep, send, width):
    own = lax.axis_index("node")
    swap_core = [(0, 1), (1, 0)]

    def swap(x, bit):
        return lax.ppermute(x, "node", [(i, i ^ bit) for i in range(slots)])

    came = lax.ppermute(send, "rep", swap_core)
    total = keep + came
    quarter = total.shape[1] // 2
    low, high = total[:, :quarter], total[:, quarter:]
    odd = own % 2 == 1
    mine = jnp.where(odd, high, low)
    other = jnp.where(odd, low, high).astype(BF16)
    mine = (mine + swap(other, 1).astype(F32)).astype(BF16)
    bit = 2
    while bit < slots:
        mine = (mine.astype(F32) + swap(mine, bit).astype(F32)).astype(BF16)
        bit *= 2
    other = swap(mine, 1)
    half = jnp.concatenate([jnp.where(odd, other, mine), jnp.where(odd, mine, other)], axis=1)
    other = lax.ppermute(half, "rep", swap_core)
    return finish(half, other, width)


def on_device(
    normed_input,
    queries,
    rotated_key_heads,
    frozen_value_rows,
    adapter_down_weight,
    adapter_up_weight,
    output_gradient,
    parents,
    lengths,
):
    x = normed_input[0]
    rows, width = x.shape
    slots = lax.axis_size("node")
    key_blocks = gather_keys(slots, rotated_key_heads[0])
    message, low, qt, gt = prepare(
        slots // 2 if paired(slots) else 1,
        lengths,
        x,
        adapter_down_weight.T,
        adapter_up_weight,
        frozen_value_rows[0],
        queries[0],
        output_gradient[0],
    )
    value_pair = gather_values(slots, message)
    projected, parts, lse = stats(slots, parents, lengths, key_blocks, qt, gt, adapter_up_weight, low)
    received = lax.all_to_all(projected, "node", 0, 0)
    factor = (slots * lax.axis_size("rep") * rows) ** (-0.5)
    keep, send = gradients(slots, received, x, parts, low, factor)
    down_grad, up_grad = sum_over_all(slots, keep, send, width)
    carried = ()
    for group in range(KEY_HEADS):
        carried = attend(slots, group, carried, parents, lengths, key_blocks, value_pair, qt, gt, lse)
    attended, query_grad = carried
    return (attended[None], query_grad[None], down_grad.T, up_grad)


def solution(mesh):
    tokens = P(("groups", "rep"), "node", None)
    trees = P(("groups", "rep"), None)
    return jax.shard_map(
        on_device,
        mesh=mesh,
        in_specs=(tokens,) * 4 + (P(), P()) + (tokens, trees, trees),
        out_specs=(tokens, tokens, P("groups", None), P("groups", None)),
        check_vma=False,
    )
```
